256 devices in a mesh: dp: 16 (over x_lo, z), space: 16 (over x_hi, y, core).
Axes of the slice: x: 4 (x_hi: 2, x_lo: 2; x = x_hi * 2 + x_lo), y: 4, z: 8, core: 2. Of those that a mesh axis runs over, the one named last changes fastest.
Arguments:
- volume_in: bfloat16 [16, 16, 16, 64, 128], P('dp', 'space'), may hold values from -6 to 6
- hidden_act: bfloat16 [16, 16, 32, 64, 128], P('dp', 'space'), may hold values from -6 to 6
- out_cot: bfloat16 [16, 16, 32, 64, 128], P('dp', 'space'), may hold values from -6 to 6
- kernel_one: bfloat16 [3, 3, 3, 16, 32], replicated, may hold values from -0.3125 to 0.3125
- kernel_two: bfloat16 [3, 3, 3, 32, 32], replicated, may hold values from -0.21875 to 0.21875
- grad_bucket: float32 [256, 524288], P(('dp', 'space')), may hold values from -1 to 1
Outputs:
- grad_input: bfloat16 [16, 16, 16, 64, 128], P('dp', 'space')
- grad_kernel_one: float32 [3, 3, 3, 16, 32], replicated
- grad_kernel_two: float32 [3, 3, 3, 32, 32], replicated
- bucket_sum: float32 [524288], replicated
The draws below stay inside these ranges and needn't reach their ends.
All inputs are finite; a program needn't handle non-finite values.
Results may differ from the reference program's by a relative error of at most 0.013.
Values may be sent and summed in bfloat16 or wider, within the bound.
A program may use at most 128 MiB of HBM per device.

```python
import math
import jax
import jax.numpy as jnp
from jax import lax

C0 = 16
C1 = 32
C2 = 32
NX = 64
NY = 128
BUCKET = 524288
SAMPLES = 16
NZ = 16
DEVICES = 256


def block_scale(own_key, dims, cuts, least, top_value):
    gain, own = 1.0, jax.random.fold_in(own_key, 6)
    for dim, parts in cuts:
        draws = jnp.exp(jax.random.uniform(jax.random.fold_in(own, dim), (parts,), jnp.float32, least / len(cuts), top_value / len(cuts)))
        gain = gain * jnp.repeat(draws, dims[dim] // parts).reshape([-1 if axis == dim else 1 for axis in range(len(dims))])
    return gain


def normal_values(own_key, extent, spread, reach, shards=(), dtype=jnp.bfloat16):
    result = jax.random.normal(own_key, extent, jnp.float32) * spread
    if len(shards) > 0:
        result = block_scale(own_key, extent, shards, -0.22, 0.18) * result
    return jnp.clip(result, min=-reach, max=reach).astype(dtype)


def setup_inputs(seed: int = 0) -> dict:
    key_of = jax.random.split(jax.random.key(seed), 7)
    volume_in = normal_values(key_of[0], (SAMPLES, NZ, C0, NX, NY), 1.0, 6.0, ((0, 16), (1, 16)))
    hidden_act = normal_values(key_of[1], (SAMPLES, NZ, C1, NX, NY), 1.0, 6.0, ((0, 16), (1, 16)))
    out_cot = normal_values(key_of[2], (SAMPLES, NZ, C2, NX, NY), 1.0, 6.0, ((0, 16), (1, 16)))
    kernel_one = normal_values(key_of[3], (3, 3, 3, C0, C1), (27 * C0) ** -0.5, 0.3125)
    kernel_two = normal_values(key_of[4], (3, 3, 3, C1, C2), (27 * C1) ** -0.5, 0.21875)
    grad_bucket = normal_values(key_of[5], (DEVICES, BUCKET), 0.0625, 1.0, ((0, 256),), jnp.float32)
    return dict(volume_in=volume_in, hidden_act=hidden_act, out_cot=out_cot, kernel_one=kernel_one, kernel_two=kernel_two, grad_bucket=grad_bucket)


def convolve(field, kernel):
    numbers = lax.ConvDimensionNumbers(lhs_spec=(0, 2, 1, 3, 4), rhs_spec=(4, 3, 0, 1, 2), out_spec=(0, 2, 1, 3, 4))
    return lax.conv_general_dilated(field.astype(jnp.float32), kernel.astype(jnp.float32), (1, 1, 1), ((1, 1), (1, 1), (1, 1)), dimension_numbers=numbers, precision=lax.Precision.HIGHEST)

def flipped(kernel):
    return jnp.swapaxes(kernel[::-1, ::-1, ::-1], 3, 4)

def kernel_terms(field, cotan):
    padded = jnp.pad(field.astype(jnp.float32), ((0, 0), (1, 1), (0, 0), (1, 1), (1, 1)))
    depth_cells, width_x, width_y = (cotan.shape[1], cotan.shape[3], cotan.shape[4])
    cot_wide = cotan.astype(jnp.float32)
    planes = []
    for along_z in range(3):
        for along_x in range(3):
            for along_y in range(3):
                window = padded[:, along_z:along_z + depth_cells, :, along_x:along_x + width_x, along_y:along_y + width_y]
                planes.append(jnp.einsum('nzcxy,nzdxy->cd', window, cot_wide, precision=lax.Precision.HIGHEST))
    return jnp.stack(planes).reshape((3, 3, 3) + planes[0].shape)

def reference(volume_in, hidden_act, out_cot, kernel_one, kernel_two, grad_bucket):

    def single(sample):
        volume, act, cotan = sample
        volume, act, cotan = (volume[None], act[None], cotan[None])
        act_grad = convolve(cotan, flipped(kernel_two))
        slope = jnp.where(act > 0, 1.0, 0.2).astype(jnp.float32)
        pre_grad = (act_grad * slope).astype(jnp.bfloat16)
        grad_in = convolve(pre_grad, flipped(kernel_one)).astype(jnp.bfloat16)
        return (grad_in[0], kernel_terms(volume, pre_grad), kernel_terms(act, cotan))
    grad_input, terms_one, terms_two = lax.map(single, (volume_in, hidden_act, out_cot))
    scale = 1.0 / math.sqrt(SAMPLES * NZ * NX * NY)
    grad_kernel_one = lax.optimization_barrier(jnp.sum(terms_one, axis=0)) * scale
    grad_kernel_two = lax.optimization_barrier(jnp.sum(terms_two, axis=0)) * scale
    bucket_sum = lax.optimization_barrier(jnp.sum(grad_bucket, axis=0))
    return (grad_input, grad_kernel_one, grad_kernel_two, bucket_sum)
```

```python
import functools
import math

import jax
import jax.numpy as jnp
from jax import lax
from jax.experimental import pallas as pl
from jax.experimental.pallas import tpu as pltpu
from jax.sharding import PartitionSpec as P

MESH = pl.DeviceIdType.MESH
F32 = jnp.float32
BF16 = jnp.bfloat16
LANES = 128
GROWS = 512


def landed(ref, sem):
    pltpu.make_async_copy(ref, ref, sem).wait()


def shifted(value, step):
    width = value.shape[-1]
    lane = lax.broadcasted_iota(jnp.int32, value.shape, value.ndim - 1)
    if step < 0:
        return jnp.where(lane >= 1, pltpu.roll(value, 1, value.ndim - 1), 0.0)
    return jnp.where(lane < width - 1, pltpu.roll(value, width - 1, value.ndim - 1), 0.0)


def relaid(raw, start, count):
    return jnp.transpose(raw[:, pl.ds(start, count), :].astype(F32), (1, 0, 2))


def weights(kernel, out, channels):
    for j in range(3):
        for k in range(3):
            pieces = [kernel[(2 - p) * 9 + (2 - j) * 3 + (2 - k)].astype(F32) for p in range(3)]
            row = (j * 3 + k) * channels
            out[row : row + channels, :] = jnp.concatenate(pieces, axis=1).astype(BF16)


def convolve(field, weight, total, width_x, channels):
    rows = 3 * channels
    total[0:2] = jnp.zeros((2, rows, LANES), F32)

    @pl.loop(0, width_x // 2)
    def _(step):
        x = step * 2
        pair = jnp.concatenate([field[x], field[x + 1]], axis=1)
        product = jnp.dot(weight[...], pair, preferred_element_type=F32)
        first, second = product[:, :LANES], product[:, LANES:]
        total[x] += first[2 * rows :]
        total[x + 1] += first[rows : 2 * rows] + second[2 * rows :]
        total[x + 2] = first[:rows] + second[rows : 2 * rows]
        total[x + 3] = second[:rows]


def gathered(total, x, channels):
    value = total[x + 1]
    return (
        value[channels : 2 * channels]
        + shifted(value[:channels], -1)
        + shifted(value[2 * channels :], 1)
    )


def kernel_terms(field, planes, out, first, width_x, channels):
    rows = 9 * channels
    depth = planes.shape[1]
    unroll = 4
    out[first : first + rows, :] = jnp.zeros((rows, LANES), F32)

    @pl.loop(0, width_x // unroll)
    def _(step):
        x = step * unroll
        left = jnp.concatenate(
            [field[pl.ds(x + u, 3)].reshape(rows, LANES) for u in range(unroll)], axis=1
        )
        right = jnp.concatenate([planes[x + u] for u in range(unroll)], axis=1)
        out[first : first + rows, :depth] += lax.dot_general(
            left, right, (((1,), (1,)), ((), ())), preferred_element_type=F32
        )


def kernel(
    n, m, scale,
    vol_hbm, act_hbm, cot_hbm, one_hbm, two_hbm, bucket_hbm,
    gin_hbm, g1_hbm, g2_hbm, bsum_hbm,
    raw_vol, raw_act, raw_cot, one_v, two_v, bucket,
    cotf, actf, volf, pref, acc_two, acc_one, gin, w_one, w_two,
    s0, r0, s1, r1, s2, r2, gath,
    gpart, gsend, grecv, gx, gfull, g1_v, g2_v,
    load_sem, out_sem, halo_send, halo_recv, b_send, b_recv, g_send, g_recv,
):
    c1, width_x, width_y = raw_act.shape
    c0, c2 = raw_vol.shape[0], raw_cot.shape[0]
    dp = lax.axis_index("dp")
    sp = lax.axis_index("space")
    half = m // 2
    core, pos = lax.rem(sp, 2), sp // 2
    rows = bucket.shape[0]
    h = rows // 2
    q = h // max(half, 1)
    e = q // n
    gr = GROWS // m

    def in_space(other):
        return (dp, other)

    def in_dp(other):
        return (other, sp)

    def remote(src, dst, send, recv, device):
        return pltpu.make_async_remote_copy(
            src_ref=src, dst_ref=dst, send_sem=send, recv_sem=recv, device_id=device, device_id_type=MESH
        )

    if n * m > 1:
        barrier = pltpu.get_barrier_semaphore()

        @pl.loop(1, m)
        def _(o):
            pl.semaphore_signal(barrier, inc=1, device_id=in_space(lax.rem(sp + o, m)), device_id_type=MESH)

        @pl.loop(1, n)
        def _(o):
            pl.semaphore_signal(barrier, inc=1, device_id=in_dp(lax.rem(dp + o, n)), device_id_type=MESH)

    loads = [
        pltpu.make_async_copy(src, dst, load_sem.at[i])
        for i, (src, dst) in enumerate(
            (
                (cot_hbm, raw_cot), (bucket_hbm, bucket), (act_hbm, raw_act),
                (two_hbm, two_v), (vol_hbm, raw_vol), (one_hbm, one_v),
            )
        )
    ]
    for load in loads:
        load.start()
    block = 16

    loads[0].wait()

    @pl.loop(0, width_x // block)
    def _(step):
        x = step * block
        cotf[pl.ds(x, block), c2 : 2 * c2, :] = relaid(raw_cot, x, block).astype(BF16)

    if n * m > 1:
        pl.semaphore_wait(barrier, m - 1 + n - 1)

    def exchange(field, depth, index):
        own = field.at[:, depth : 2 * depth, :]
        lower, upper = field.at[:, 0:depth, :], field.at[:, 2 * depth : 3 * depth, :]
        up = remote(own, lower, halo_send.at[index, 0], halo_recv.at[index, 0], in_space(lax.rem(sp + 1, m)))
        down = remote(own, upper, halo_send.at[index, 1], halo_recv.at[index, 1], in_space(lax.rem(sp + m - 1, m)))

        @pl.when(sp < m - 1)
        def _():
            up.start()

        @pl.when(sp > 0)
        def _():
            down.start()

        def arrive():
            @pl.when(sp > 0)
            def _():
                landed(lower, halo_recv.at[index, 0])

            @pl.when(sp < m - 1)
            def _():
                landed(upper, halo_recv.at[index, 1])

        def sent():
            @pl.when(sp < m - 1)
            def _():
                landed(own, halo_send.at[index, 0])

            @pl.when(sp > 0)
            def _():
                landed(own, halo_send.at[index, 1])

        return arrive, sent

    def blank(field, depth):
        @pl.when(sp == 0)
        def _():
            @pl.loop(0, width_x)
            def _(x):
                field[x, 0:depth, :] = jnp.zeros((depth, LANES), BF16)

        @pl.when(sp == m - 1)
        def _():
            @pl.loop(0, width_x)
            def _(x):
                field[x, 2 * depth : 3 * depth, :] = jnp.zeros((depth, LANES), BF16)

    cot_arrive, cot_sent = exchange(cotf, c2, 0)
    blank(cotf, c2)
    blank(pref, c1)

    part = 256

    loads[1].wait()
    partner = in_space(sp + 1 - 2 * core)
    if m > 1:
        far = (1 - core) * h
        near = core * h

        @pl.loop(0, h // part)
        def _(t):
            s0[pl.ds(t * part, part), :] = bucket[pl.ds(pl.multiple_of(far + t * part, part), part), :].astype(BF16)

        remote(s0, r0, b_send.at[0], b_recv.at[0], partner).start()

    def spread(raw, field, channels):
        zero = jnp.zeros((3 * channels, LANES), BF16)
        field[0] = zero
        field[width_x + 1] = zero

        @pl.loop(0, width_x // block)
        def _(step):
            x = step * block
            value = relaid(raw, x, block).reshape(block * channels, LANES)
            for k in range(3):
                moved = value if k == 1 else shifted(value, k - 1)
                field[pl.ds(x + 1, block), k * channels : (k + 1) * channels, :] = moved.astype(BF16).reshape(
                    block, channels, LANES
                )

    loads[2].wait()
    spread(raw_act, actf, c1)
    loads[3].wait()
    weights(two_v, w_two, c1)

    if m > 1:
        landed(r0, b_recv.at[0])

        @pl.loop(0, h // part)
        def _(t):
            at = pl.ds(pl.multiple_of(near + t * part, part), part)
            value = bucket[at, :] + r0[pl.ds(t * part, part), :].astype(F32)
            bucket[at, :] = value
            s1[pl.ds(t * part, part), :] = value.astype(BF16)

        @pl.loop(1, half)
        def _(o):
            other = lax.rem(pos + o, half)
            remote(
                s1.at[pl.ds(pl.multiple_of(other * q, q), q), :], r1.at[o - 1],
                b_send.at[1], b_recv.at[1], in_space(other * 2 + core),
            ).start()

    loads[4].wait()
    spread(raw_vol, volf, c0)
    loads[5].wait()
    weights(one_v, w_one, c0)

    if m > 1:
        cot_arrive()
    convolve(cotf, w_two, acc_two, width_x, c1)

    @pl.loop(0, width_x // 2)
    def _(step):
        for u in range(2):
            x = step * 2 + u
            slope = jnp.where(actf[x + 1, c1 : 2 * c1, :].astype(F32) > 0, 1.0, 0.2)
            pref[x, c1 : 2 * c1, :] = (gathered(acc_two, x, c1) * slope).astype(BF16)

    pre_arrive, pre_sent = exchange(pref, c1, 1)

    mine = core * h + pos * q
    if m > 1:
        if half > 1:
            landed(r1, b_recv.at[1])
        own = pl.ds(pl.multiple_of(mine, q), q)
        value = bucket[own, :]
        for o in range(1, half):
            value = value + r1[o - 1].astype(F32)
        bucket[own, :] = value
        s2[...] = value.astype(BF16)

        @pl.loop(1, n)
        def _(o):
            other = lax.rem(dp + o, n)
            remote(
                s2.at[pl.ds(pl.multiple_of(other * e, e), e), :], r2.at[o - 1],
                b_send.at[2], b_recv.at[2], in_dp(other),
            ).start()

    kernel_terms(actf, cotf, gpart, 0, width_x, c1)

    if m > 1:
        landed(r2, b_recv.at[2])
        start = pl.multiple_of(mine + dp * e, e)
        value = bucket[pl.ds(start, e), :]
        for o in range(1, n):
            value = value + r2[o - 1].astype(F32)
        own_rows = gath.at[pl.ds(start, e), :]
        own_rows[...] = value.astype(BF16)

        @pl.loop(1, n)
        def _(o):
            remote(own_rows, own_rows, b_send.at[3], b_recv.at[3], in_dp(lax.rem(dp + o, n))).start()

    if m > 1:
        pre_arrive()
    kernel_terms(volf, pref, gpart, 9 * c1, width_x, c0)
    used = 9 * (c1 + c0)
    gpart[used:, :] = jnp.zeros((GROWS - used, LANES), F32)

    if m > 1:
        gsend[...] = gpart[...].astype(gsend.dtype)

        @pl.loop(1, m)
        def _(o):
            other = lax.rem(sp + o, m)
            remote(
                gsend.at[pl.ds(pl.multiple_of(other * gr, gr), gr), :], grecv.at[o - 1],
                g_send.at[0], g_recv.at[0], in_space(other),
            ).start()

        landed(gath.at[pl.ds(0, (n - 1) * e), :], b_recv.at[3])
        own_part = gath.at[pl.ds(pl.multiple_of(mine, q), q), :]

        @pl.loop(1, half)
        def _(o):
            other = lax.rem(pos + o, half)
            remote(own_part, own_part, b_send.at[4], b_recv.at[4], in_space(other * 2 + core)).start()

    convolve(pref, w_one, acc_one, width_x, c0)

    @pl.loop(0, width_x // 4)
    def _(step):
        for u in range(4):
            x = step * 4 + u
            gin[x] = gathered(acc_one, x, c0).astype(BF16)

    gin_out = pltpu.make_async_copy(gin, gin_hbm, out_sem.at[0])
    gin_out.start()

    if m > 1:
        landed(grecv, g_recv.at[0])
        value = gpart[pl.ds(pl.multiple_of(sp * gr, gr), gr), :]
        for o in range(1, m):
            value = value + grecv[o - 1].astype(F32)
        gx[dp] = value.astype(gx.dtype)

        @pl.loop(1, n)
        def _(o):
            remote(gx.at[dp], gx.at[dp], g_send.at[1], g_recv.at[1], in_dp(lax.rem(dp + o, n))).start()

        if half > 1:
            landed(gath.at[pl.ds(0, (half - 1) * q), :], b_recv.at[4])
        own_half = gath.at[pl.ds(pl.multiple_of(near, h), h), :]
        remote(own_half, own_half, b_send.at[5], b_recv.at[5], partner).start()

        landed(gx.at[pl.ds(0, n - 1)], g_recv.at[1])
        value = gx[0].astype(F32)
        for d in range(1, n):
            value = value + gx[d].astype(F32)
        own_rows_g = gfull.at[pl.ds(pl.multiple_of(sp * gr, gr), gr), :]
        own_rows_g[...] = (value * scale).astype(gfull.dtype)

        @pl.loop(1, m)
        def _(o):
            remote(own_rows_g, own_rows_g, g_send.at[2], g_recv.at[2], in_space(lax.rem(sp + o, m))).start()

        landed(gath.at[pl.ds(0, h), :], b_recv.at[5])
    bsum_out = pltpu.make_async_copy(gath, bsum_hbm, out_sem.at[1])
    bsum_out.start()
    if m > 1:
        landed(gfull.at[pl.ds(0, (m - 1) * gr), :], g_recv.at[2])

    for j in range(3):
        for k in range(3):
            for p in range(3):
                at = (2 - p) * 9 + j * 3 + k
                row = (j * 3 + k) * c1
                g2_v[at] = gfull[row : row + c1, p * c2 : (p + 1) * c2].astype(F32)
                row = 9 * c1 + (j * 3 + k) * c0
                g1_v[at] = gfull[row : row + c0, p * c1 : (p + 1) * c1].astype(F32)
    g2_out = pltpu.make_async_copy(g2_v, g2_hbm, out_sem.at[2])
    g1_out = pltpu.make_async_copy(g1_v, g1_hbm, out_sem.at[3])
    g2_out.start()
    g1_out.start()

    if m > 1:
        cot_sent()
        pre_sent()
        landed(s0, b_send.at[0])
        if half > 1:
            landed(r1, b_send.at[1])
            landed(gath.at[pl.ds(0, (half - 1) * q), :], b_send.at[4])
        landed(r2, b_send.at[2])
        landed(gath.at[pl.ds(0, (n - 1) * e), :], b_send.at[3])
        landed(gath.at[pl.ds(0, h), :], b_send.at[5])
        landed(grecv, g_send.at[0])
        landed(gx.at[pl.ds(0, n - 1)], g_send.at[1])
        landed(gfull.at[pl.ds(0, (m - 1) * gr), :], g_send.at[2])
    gin_out.wait()
    bsum_out.wait()
    g2_out.wait()
    g1_out.wait()


def call(n, m, scale, vol, act, cot, one, two, bucket):
    c0, width_x, width_y = vol.shape
    c1, c2 = act.shape[0], cot.shape[0]
    rows = bucket.shape[0]
    half = max(m // 2, 1)
    h = rows // 2
    q = h // half
    e = q // n
    gr = GROWS // m
    wire = BF16
    vmem = pltpu.VMEM
    scratch = [
        vmem((c0, width_x, width_y), BF16), vmem((c1, width_x, width_y), BF16), vmem((c2, width_x, width_y), BF16),
        vmem((27, c0, c1), BF16), vmem((27, c1, c2), BF16), vmem((rows, LANES), F32),
        vmem((width_x, 3 * c2, LANES), BF16), vmem((width_x + 2, 3 * c1, LANES), BF16),
        vmem((width_x + 2, 3 * c0, LANES), BF16), vmem((width_x, 3 * c1, LANES), BF16),
        vmem((width_x + 2, 3 * c1, LANES), F32), vmem((width_x + 2, 3 * c0, LANES), F32),
        vmem((width_x, c0, LANES), BF16),
        vmem((9 * c0, 3 * c1), BF16), vmem((9 * c1, 3 * c2), BF16),
        vmem((h, LANES), BF16), vmem((h, LANES), BF16), vmem((h, LANES), BF16),
        vmem((max(half - 1, 1), q, LANES), BF16), vmem((q, LANES), BF16), vmem((max(n - 1, 1), e, LANES), BF16),
        vmem((rows, LANES), BF16),
        vmem((GROWS, LANES), F32), vmem((GROWS, LANES), wire), vmem((max(m - 1, 1), gr, LANES), wire),
        vmem((n, gr, LANES), wire), vmem((GROWS, LANES), wire),
        vmem((27, c0, c1), F32), vmem((27, c1, c2), F32),
        pltpu.SemaphoreType.DMA((6,)), pltpu.SemaphoreType.DMA((4,)),
        pltpu.SemaphoreType.DMA((2, 2)), pltpu.SemaphoreType.DMA((2, 2)),
        pltpu.SemaphoreType.DMA((6,)), pltpu.SemaphoreType.DMA((6,)),
        pltpu.SemaphoreType.DMA((3,)), pltpu.SemaphoreType.DMA((3,)),
    ]
    hbm = pl.BlockSpec(memory_space=pltpu.HBM)
    cells = width_x * width_y
    return pl.pallas_call(
        functools.partial(kernel, n, m, scale),
        out_shape=(
            jax.ShapeDtypeStruct((width_x, c0, width_y), BF16),
            jax.ShapeDtypeStruct((27, c0, c1), F32),
            jax.ShapeDtypeStruct((27, c1, c2), F32),
            jax.ShapeDtypeStruct((rows, LANES), BF16),
        ),
        in_specs=[hbm] * 6,
        out_specs=(hbm,) * 4,
        scratch_shapes=scratch,
        compiler_params=pltpu.CompilerParams(
            collective_id=0 if n * m > 1 else None, has_side_effects=True, vmem_limit_bytes=64 << 20
        ),
        cost_estimate=pl.CostEstimate(
            flops=4 * 27 * cells * c1 * (c0 + c2), bytes_accessed=8 << 20, transcendentals=0
        ),
    )(vol, act, cot, one, two, bucket)


def per_device(n, m, volume_in, hidden_act, out_cot, kernel_one, kernel_two, grad_bucket):
    c0, width_x, width_y = volume_in.shape[2:]
    c1 = hidden_act.shape[2]
    scale = 1.0 / math.sqrt(volume_in.shape[0] * n * volume_in.shape[1] * m * width_x * width_y)
    gin, g1, g2, bsum = call(
        n, m, scale,
        volume_in[0, 0], hidden_act[0, 0], out_cot[0, 0],
        kernel_one.reshape((27,) + kernel_one.shape[3:]), kernel_two.reshape((27,) + kernel_two.shape[3:]),
        grad_bucket.reshape(-1, LANES),
    )
    gin = jnp.transpose(gin, (1, 0, 2))[None, None]
    return (
        gin, g1.reshape(kernel_one.shape), g2.reshape(kernel_two.shape), bsum.astype(F32).reshape(-1),
    )


def solution(mesh):
    fields = P("dp", "space", None, None, None)
    return jax.shard_map(
        functools.partial(per_device, mesh.shape["dp"], mesh.shape["space"]),
        mesh=mesh,
        in_specs=(fields, fields, fields, P(), P(), P(("dp", "space"), None)),
        out_specs=(fields, P(), P(), P()),
        check_vma=False,
    )
```

```python
import functools
import math

import jax
import jax.numpy as jnp
from jax import lax
from jax.experimental import pallas as pl
from jax.experimental.pallas import tpu as pltpu
from jax.sharding import PartitionSpec as P

MESH = pl.DeviceIdType.MESH
F32 = jnp.float32
BF16 = jnp.bfloat16
LANES = 128
GROWS = 512
UNROLL = 16
COUNT = 8
VMEM_LIMIT = 40 << 20


def landed(ref, sem):
    pltpu.make_async_copy(ref, ref, sem).wait()


def shifted(value, step):
    width = value.shape[-1]
    lane = lax.broadcasted_iota(jnp.int32, value.shape, value.ndim - 1)
    if step < 0:
        return jnp.where(lane >= 1, pltpu.roll(value, 1, value.ndim - 1), 0.0)
    return jnp.where(lane < width - 1, pltpu.roll(value, width - 1, value.ndim - 1), 0.0)


def relaid(raw, start, count):
    return jnp.transpose(raw[:, pl.ds(start, count), :].astype(F32), (1, 0, 2))


def weights(kernel, out, channels):
    for k in range(3):
        pieces = [
            kernel[(2 - p) * 9 + (2 - j) * 3 + (2 - k)].astype(F32) for j in range(3) for p in range(3)
        ]
        out[k * channels : (k + 1) * channels, :] = jnp.concatenate(pieces, axis=1).astype(BF16)


def convolved(field, weight, x, count, channels):
    rows = weight.shape[1]
    columns = [field[pl.ds(x + u, 3)].reshape(rows, LANES) for u in range(count)]
    product = jnp.dot(weight[...], jnp.concatenate(columns, axis=1), preferred_element_type=F32)
    out = []
    for u in range(count):
        value = product[:, u * LANES : (u + 1) * LANES]
        out.append(
            value[channels : 2 * channels]
            + shifted(value[:channels], -1)
            + shifted(value[2 * channels :], 1)
        )
    return out


def kernel_terms(left, right, offset, out, first, low, high, unroll):
    rows = 3 * left.shape[1]
    depth = right.shape[1]

    @pl.loop(0, (high - low) // unroll)
    def _(step):
        x = low + step * unroll
        a = jnp.concatenate([left[pl.ds(x + u, 3)].reshape(rows, LANES) for u in range(unroll)], axis=1)
        b = jnp.concatenate([right[x + u + offset] for u in range(unroll)], axis=1)
        out[first : first + rows, :depth] += lax.dot_general(
            a, b, (((1,), (1,)), ((), ())), preferred_element_type=F32
        )


def kernel(
    n, m, scale,
    vol_hbm, act_hbm, cot_hbm, one_hbm, two_hbm, bucket_hbm,
    gin, gfull, gath,
    raw_vol, raw_act, raw_cot, one_v, two_v, bucket,
    cotf, actf, volf, pref, turned, w_one, w_two,
    r0, s1, r1, s2, r2,
    gpart, gsend, grecv, gx,
    load_sem, halo_send, halo_recv, b_send, b_recv, c_recv, g_send, g_recv,
):
    c1, width_x, width_y = raw_act.shape
    c0, c2 = raw_vol.shape[0], raw_cot.shape[0]
    dp = lax.axis_index("dp")
    sp = lax.axis_index("space")
    half = max(m // 2, 1)
    core, pos = lax.rem(sp, 2), sp // 2
    h = bucket.shape[0]
    q = h // half
    e = q // n
    gr = GROWS // m
    near, far = core * h, (1 - core) * h
    mine = near + pos * q
    partner = (dp, sp + 1 - 2 * core)

    def in_space(other):
        return (dp, other)

    def in_dp(other):
        return (other, sp)

    def remote(src, dst, send, recv, device):
        return pltpu.make_async_remote_copy(
            src_ref=src, dst_ref=dst, send_sem=send, recv_sem=recv, device_id=device, device_id_type=MESH
        )

    if n * m > 1:
        barrier = pltpu.get_barrier_semaphore()

        @pl.loop(1, m)
        def _(o):
            pl.semaphore_signal(barrier, inc=1, device_id=in_space(lax.rem(sp + o, m)), device_id_type=MESH)

        @pl.loop(1, n)
        def _(o):
            pl.semaphore_signal(barrier, inc=1, device_id=in_dp(lax.rem(dp + o, n)), device_id_type=MESH)

    loads = [
        pltpu.make_async_copy(src, dst, load_sem.at[i])
        for i, (src, dst) in enumerate(
            (
                (cot_hbm, raw_cot), (vol_hbm, raw_vol), (act_hbm, raw_act),
                (two_hbm, two_v), (one_hbm, one_v), (bucket_hbm.at[pl.ds(pl.multiple_of(near, h), h), :], bucket),
            )
        )
    ]
    for load in loads:
        load.start()
    block = 16

    for field in (cotf, actf, volf, pref):
        for slot in (0, width_x + 1):
            field[slot] = jnp.zeros(field.shape[1:], BF16)
    gpart[...] = jnp.zeros(gpart.shape, F32)

    def center(raw, field, channels):
        @pl.loop(0, width_x // block)
        def _(step):
            x = step * block
            field[pl.ds(x + 1, block), channels : 2 * channels, :] = relaid(raw, x, block).astype(BF16)

    def spread(raw, field, channels):
        @pl.loop(0, width_x // block)
        def _(step):
            x = step * block
            value = relaid(raw, x, block).reshape(block * channels, LANES)
            for k in range(3):
                moved = value if k == 1 else shifted(value, k - 1)
                field[pl.ds(x + 1, block), k * channels : (k + 1) * channels, :] = moved.astype(BF16).reshape(
                    block, channels, LANES
                )

    def planes(field, low, high):
        depth = field.shape[1] // 3
        return [field.at[low + 1 : high + 1, p * depth : (p + 1) * depth, :] for p in range(3)]

    def send_halo(field, low, high, index):
        lower, own, upper = planes(field, low, high)

        @pl.when(sp < m - 1)
        def _():
            remote(own, lower, halo_send.at[index, 0], halo_recv.at[index, 0], in_space(lax.rem(sp + 1, m))).start()

        @pl.when(sp > 0)
        def _():
            remote(own, upper, halo_send.at[index, 1], halo_recv.at[index, 1], in_space(lax.rem(sp + m - 1, m))).start()

    def have_halo(field, low, high, index):
        lower, own, upper = planes(field, low, high)

        @pl.when(sp > 0)
        def _():
            landed(lower, halo_recv.at[index, 0])

        @pl.when(sp < m - 1)
        def _():
            landed(upper, halo_recv.at[index, 1])

    def sent_halo(field, low, high, index):
        lower, own, upper = planes(field, low, high)

        @pl.when(sp < m - 1)
        def _():
            landed(own, halo_send.at[index, 0])

        @pl.when(sp > 0)
        def _():
            landed(own, halo_send.at[index, 1])

    def blank(field):
        depth = field.shape[1] // 3
        for edge, p in ((0, 0), (m - 1, 2)):

            @pl.when(sp == edge)
            def _():
                @pl.loop(1, width_x + 1)
                def _(x):
                    field[x, p * depth : (p + 1) * depth, :] = jnp.zeros((depth, LANES), BF16)

    pieces = 4
    length = width_x // pieces
    raw_cuts = [(c * length, (c + 1) * length) for c in range(pieces)]
    pre_cuts = [
        (max(low - COUNT, 0), high if c == pieces - 1 else high - COUNT) for c, (low, high) in enumerate(raw_cuts)
    ]

    loads[0].wait()
    center(raw_cot, cotf, c2)
    if n * m > 1:
        pl.semaphore_wait(barrier, m - 1 + n - 1)
        for c, (low, high) in enumerate(raw_cuts):
            send_halo(cotf, low, high, c)
        remote(bucket_hbm.at[pl.ds(pl.multiple_of(far, h), h), :], r0, b_send.at[0], b_recv.at[0], partner).start()
    blank(cotf)
    blank(volf)
    blank(pref)
    loads[1].wait()
    center(raw_vol, volf, c0)
    if n * m > 1:
        send_halo(volf, 0, width_x, 2 * pieces)
    loads[2].wait()
    spread(raw_act, actf, c1)
    loads[3].wait()
    weights(two_v, w_two, c1)
    loads[4].wait()
    weights(one_v, w_one, c0)
    loads[5].wait()

    part = min(256, h)
    if m > 1:
        landed(r0, b_recv.at[0])

        @pl.loop(0, h // part)
        def _(t):
            at = pl.ds(t * part, part)
            value = bucket[at, :] + r0[at, :]
            bucket[at, :] = value
            s1[at, :] = value.astype(BF16)

        @pl.loop(1, half)
        def _(o):
            other = lax.rem(pos + o, half)
            remote(
                s1.at[pl.ds(pl.multiple_of(other * q, q), q), :], r1.at[o - 1],
                b_send.at[1], b_recv.at[1], in_space(other * 2 + core),
            ).start()

    def third():
        if half > 1:
            landed(r1, b_recv.at[1])
        own = pl.ds(pl.multiple_of(pos * q, q), q)
        value = bucket[own, :]
        for o in range(1, half):
            value = value + r1[o - 1].astype(F32)
        bucket[own, :] = value
        s2[...] = value.astype(BF16)

        @pl.loop(1, n)
        def _(o):
            other = lax.rem(dp + o, n)
            remote(
                s2.at[pl.ds(pl.multiple_of(other * e, e), e), :], r2.at[o - 1],
                b_send.at[2], b_recv.at[2], in_dp(other),
            ).start()

    for c in range(pieces):
        low, high = pre_cuts[c]
        if m > 1:
            have_halo(cotf, *raw_cuts[c], c)

        @pl.loop(0, (high - low) // COUNT)
        def _(step):
            x = low + step * COUNT
            for u, value in enumerate(convolved(cotf, w_two, x, COUNT, c1)):
                slope = jnp.where(actf[x + u + 1, c1 : 2 * c1, :].astype(F32) > 0, 1.0, 0.2)
                value = (value * slope).astype(BF16)
                pref[x + u + 1, c1 : 2 * c1, :] = value
                wide = value.astype(F32)
                turned[x + u, :c1, :] = shifted(wide, 1).astype(BF16)
                turned[x + u, c1 : 2 * c1, :] = value
                turned[x + u, 2 * c1 :, :] = shifted(wide, -1).astype(BF16)

        if m > 1:
            send_halo(pref, low, high, pieces + c)
            if c == 2:
                third()
        kernel_terms(actf, cotf, 1, gpart, 0, *raw_cuts[c], UNROLL)

    if m > 1:
        have_halo(volf, 0, width_x, 2 * pieces)
    kernel_terms(volf, turned, 0, gpart, 9 * c1, 0, width_x, UNROLL)

    if m > 1:
        gsend[...] = gpart[...].astype(gsend.dtype)

        @pl.loop(1, m)
        def _(o):
            other = lax.rem(sp + o, m)
            remote(
                gsend.at[pl.ds(pl.multiple_of(other * gr, gr), gr), :], grecv.at[o - 1],
                g_send.at[0], g_recv.at[0], in_space(other),
            ).start()

        landed(r2, b_recv.at[2])
        value = bucket[pl.ds(pl.multiple_of(pos * q + dp * e, e), e), :]
        for o in range(1, n):
            value = value + r2[o - 1].astype(F32)
        own_rows = gath.at[pl.ds(pl.multiple_of(mine + dp * e, e), e), :]
        own_rows[...] = value.astype(BF16)

        @pl.loop(1, n)
        def _(o):
            remote(own_rows, own_rows, b_send.at[3], b_recv.at[3], in_dp(lax.rem(dp + o, n))).start()

    def second(low, high):
        @pl.loop(0, (high - low) // COUNT)
        def _(step):
            x = low + step * COUNT
            for u, value in enumerate(convolved(pref, w_one, x, COUNT, c0)):
                gin[x + u] = value.astype(BF16)

    if m > 1:
        for c in range(pieces):
            have_halo(pref, *pre_cuts[c], pieces + c)
    second(0, width_x)

    if m > 1:
        landed(grecv, g_recv.at[0])
        value = gpart[pl.ds(pl.multiple_of(sp * gr, gr), gr), :]
        for o in range(1, m):
            value = value + grecv[o - 1].astype(F32)
        gx[dp] = value.astype(gx.dtype)

        @pl.loop(1, n)
        def _(o):
            remote(gx.at[dp], gx.at[dp], g_send.at[1], g_recv.at[1], in_dp(lax.rem(dp + o, n))).start()

        def rows_of(chip):
            return gath.at[pl.ds(pl.multiple_of(near + chip * q, q), q), :]

        landed(gath.at[pl.ds(0, (n - 1) * e), :], b_recv.at[3])

        @pl.loop(1, half)
        def _(o):
            other = lax.rem(pos + o, half)
            remote(rows_of(pos), rows_of(pos), b_send.at[4], c_recv.at[o - 1], in_space(other * 2 + core)).start()

        remote(rows_of(pos), rows_of(pos), b_send.at[5], b_recv.at[5], partner).start()

        landed(gx.at[pl.ds(0, n - 1)], g_recv.at[1])
        value = gx[0].astype(F32)
        for d in range(1, n):
            value = value + gx[d].astype(F32)
        own_g = gfull.at[pl.ds(pl.multiple_of(sp * gr, gr), gr), :]
        own_g[...] = (value * scale).astype(gfull.dtype)

        @pl.loop(1, m)
        def _(o):
            remote(own_g, own_g, g_send.at[2], g_recv.at[2], in_space(lax.rem(sp + o, m))).start()

        @pl.loop(1, half)
        def _(o):
            chip = lax.rem(pos + half - o, half)
            landed(rows_of(chip), c_recv.at[o - 1])
            remote(rows_of(chip), rows_of(chip), b_send.at[5], b_recv.at[5], partner).start()

        landed(gfull.at[pl.ds(0, (m - 1) * gr), :], g_recv.at[2])
        landed(gath.at[pl.ds(0, h), :], b_recv.at[5])

        for c in range(pieces):
            sent_halo(cotf, *raw_cuts[c], c)
            sent_halo(pref, *pre_cuts[c], pieces + c)
        sent_halo(volf, 0, width_x, 2 * pieces)
        landed(r0, b_send.at[0])
        if half > 1:
            landed(r1, b_send.at[1])
            landed(gath.at[pl.ds(0, (half - 1) * q), :], b_send.at[4])
        landed(r2, b_send.at[2])
        landed(gath.at[pl.ds(0, (n - 1) * e), :], b_send.at[3])
        landed(gath.at[pl.ds(0, h), :], b_send.at[5])
        landed(grecv, g_send.at[0])
        landed(gx.at[pl.ds(0, n - 1)], g_send.at[1])
        landed(gfull.at[pl.ds(0, (m - 1) * gr), :], g_send.at[2])


def finish(gin, gfull, gath, gin_hbm, g1_hbm, g2_hbm, bsum_hbm, gin_v, g1_v, g2_v, bsum_v, sem):
    width_x, c0, _ = gin.shape
    c1, c2 = g2_v.shape[1:]
    rows = gath.shape[0]
    count = 8
    part = rows // count
    copies = []
    for t in range(count):
        at = pl.ds(t * part, part)
        bsum_v[at, :] = gath[at, :].astype(F32)
        copies.append(pltpu.make_async_copy(bsum_v.at[at, :], bsum_hbm.at[at, :], sem.at[t]))
        copies[-1].start()
    block = 16
    for t in range(width_x // block):
        at = pl.ds(t * block, block)
        gin_v[:, at, :] = jnp.transpose(gin[at].astype(F32), (1, 0, 2)).astype(BF16)
    copies.append(pltpu.make_async_copy(gin_v, gin_hbm, sem.at[count]))
    copies[-1].start()
    for j in range(3):
        for k in range(3):
            for p in range(3):
                row = (j * 3 + k) * c1
                g2_v[(2 - p) * 9 + j * 3 + k] = gfull[row : row + c1, p * c2 : (p + 1) * c2].astype(F32)
                row = 9 * c1 + (j * 3 + p) * c0
                g1_v[p * 9 + j * 3 + k] = gfull[row : row + c0, k * c1 : (k + 1) * c1].astype(F32)
    copies.append(pltpu.make_async_copy(g2_v, g2_hbm, sem.at[count + 1]))
    copies.append(pltpu.make_async_copy(g1_v, g1_hbm, sem.at[count + 2]))
    copies[-2].start()
    copies[-1].start()
    for copy in copies:
        copy.wait()


def call(n, m, scale, vol, act, cot, one, two, bucket):
    c0, width_x, width_y = vol.shape
    c1, c2 = act.shape[0], cot.shape[0]
    rows = bucket.shape[0]
    half = max(m // 2, 1)
    h = rows // 2
    q = h // half
    e = q // n
    gr = GROWS // m
    wire = BF16
    vmem = pltpu.VMEM
    dma = pltpu.SemaphoreType.DMA
    tall = width_x + 2
    scratch = [
        vmem((c0, width_x, width_y), BF16), vmem((c1, width_x, width_y), BF16), vmem((c2, width_x, width_y), BF16),
        vmem((27, c0, c1), BF16), vmem((27, c1, c2), BF16), vmem((h, LANES), F32),
        vmem((tall, 3 * c2, LANES), BF16), vmem((tall, 3 * c1, LANES), BF16),
        vmem((tall, 3 * c0, LANES), BF16), vmem((tall, 3 * c1, LANES), BF16),
        vmem((width_x, 3 * c1, LANES), BF16),
        vmem((3 * c0, 9 * c1), BF16), vmem((3 * c1, 9 * c2), BF16),
        vmem((h, LANES), F32), vmem((h, LANES), BF16),
        vmem((max(half - 1, 1), q, LANES), BF16), vmem((q, LANES), BF16), vmem((max(n - 1, 1), e, LANES), BF16),
        vmem((GROWS, LANES), F32), vmem((GROWS, LANES), wire), vmem((max(m - 1, 1), gr, LANES), wire),
        vmem((n, gr, LANES), wire),
        dma((6,)), dma((9, 2)), dma((9, 2)), dma((6,)), dma((6,)), dma((max(half - 1, 1),)), dma((3,)), dma((3,)),
    ]
    hbm = pl.BlockSpec(memory_space=pltpu.HBM)
    local = pl.BlockSpec(memory_space=pltpu.VMEM)
    cells = width_x * width_y
    operands = [pltpu.with_memory_space_constraint(v, pltpu.HBM) for v in (vol, act, cot, one, two, bucket)]
    gin, gfull, gath = pl.pallas_call(
        functools.partial(kernel, n, m, scale),
        out_shape=(
            jax.ShapeDtypeStruct((width_x, c0, width_y), BF16),
            jax.ShapeDtypeStruct((GROWS, LANES), wire),
            jax.ShapeDtypeStruct((rows, LANES), BF16),
        ),
        in_specs=[hbm] * 6,
        out_specs=(local,) * 3,
        scratch_shapes=scratch,
        compiler_params=pltpu.CompilerParams(
            collective_id=0 if n * m > 1 else None, has_side_effects=True, vmem_limit_bytes=VMEM_LIMIT
        ),
        cost_estimate=pl.CostEstimate(
            flops=4 * 27 * cells * c1 * (c0 + c2), bytes_accessed=8 << 20, transcendentals=0
        ),
    )(*operands)
    return pl.pallas_call(
        finish,
        out_shape=(
            jax.ShapeDtypeStruct((c0, width_x, width_y), BF16),
            jax.ShapeDtypeStruct((27, c0, c1), F32),
            jax.ShapeDtypeStruct((27, c1, c2), F32),
            jax.ShapeDtypeStruct((rows, LANES), F32),
        ),
        in_specs=[local] * 3,
        out_specs=(hbm,) * 4,
        scratch_shapes=[
            vmem((c0, width_x, width_y), BF16), vmem((27, c0, c1), F32), vmem((27, c1, c2), F32),
            vmem((rows, LANES), F32), dma((11,)),
        ],
        compiler_params=pltpu.CompilerParams(vmem_limit_bytes=VMEM_LIMIT),
        cost_estimate=pl.CostEstimate(flops=0, bytes_accessed=5 << 20, transcendentals=0),
    )(gin, gfull, gath)


def per_device(n, m, volume_in, hidden_act, out_cot, kernel_one, kernel_two, grad_bucket):
    width_x, width_y = volume_in.shape[3:]
    scale = 1.0 / math.sqrt(volume_in.shape[0] * n * volume_in.shape[1] * m * width_x * width_y)
    gin, g1, g2, bsum = call(
        n, m, scale,
        volume_in[0, 0], hidden_act[0, 0], out_cot[0, 0],
        kernel_one.reshape((27,) + kernel_one.shape[3:]), kernel_two.reshape((27,) + kernel_two.shape[3:]),
        grad_bucket.reshape(-1, LANES),
    )
    return (gin[None, None], g1.reshape(kernel_one.shape), g2.reshape(kernel_two.shape), bsum.reshape(-1))


def solution(mesh):
    fields = P("dp", "space", None, None, None)
    return jax.shard_map(
        functools.partial(per_device, mesh.shape["dp"], mesh.shape["space"]),
        mesh=mesh,
        in_specs=(fields, fields, fields, P(), P(), P(("dp", "space"), None)),
        out_specs=(fields, P(), P(), P()),
        check_vma=False,
    )
```

```python
import functools
import math

import jax
import jax.numpy as jnp
from jax import lax
from jax.experimental import pallas as pl
from jax.experimental.pallas import tpu as pltpu
from jax.sharding import PartitionSpec as P

MESH = pl.DeviceIdType.MESH
F32 = jnp.float32
BF16 = jnp.bfloat16
LANES = 128
GROWS = 512
UNROLL = 16
COUNT = 8
PARTS = 2
TILE = 8
VMEM_LIMIT = 40 << 20


def landed(ref, sem):
    pltpu.make_async_copy(ref, ref, sem).wait()


def shifted(value, step):
    width = value.shape[-1]
    lane = lax.broadcasted_iota(jnp.int32, value.shape, value.ndim - 1)
    if step < 0:
        return jnp.where(lane >= 1, pltpu.roll(value, 1, value.ndim - 1), 0.0)
    return jnp.where(lane < width - 1, pltpu.roll(value, width - 1, value.ndim - 1), 0.0)


def relaid(raw, start, count):
    return jnp.transpose(raw[:, pl.ds(start, count), :].astype(F32), (1, 0, 2))


def weights(kernel, out, channels):
    for k in range(3):
        pieces = [
            kernel[(2 - p) * 9 + (2 - j) * 3 + (2 - k)].astype(F32) for j in range(3) for p in range(3)
        ]
        out[k * channels : (k + 1) * channels, :] = jnp.concatenate(pieces, axis=1).astype(BF16)


def convolved(field, weight, x, count, channels):
    rows = weight.shape[1]
    columns = [field[pl.ds(x + u, 3)].reshape(rows, LANES) for u in range(count)]
    product = jnp.dot(weight[...], jnp.concatenate(columns, axis=1), preferred_element_type=F32)
    out = []
    for u in range(count):
        value = product[:, u * LANES : (u + 1) * LANES]
        out.append(
            value[channels : 2 * channels]
            + shifted(value[:channels], -1)
            + shifted(value[2 * channels :], 1)
        )
    return out


def kernel_terms(left, right, offset, out, first, low, high, unroll):
    rows = 3 * left.shape[1]
    depth = right.shape[1]

    @pl.loop(0, (high - low) // unroll)
    def _(step):
        x = low + step * unroll
        a = jnp.concatenate([left[pl.ds(x + u, 3)].reshape(rows, LANES) for u in range(unroll)], axis=1)
        b = jnp.concatenate([right[x + u + offset] for u in range(unroll)], axis=1)
        out[first : first + rows, :depth] += lax.dot_general(
            a, b, (((1,), (1,)), ((), ())), preferred_element_type=F32
        )


def kernel(
    n, m, scale,
    vol_hbm, act_hbm, cot_hbm, one_hbm, two_hbm, bucket_hbm,
    gin, gfull, gath,
    raw_vol, raw_act, raw_cot, one_v, two_v, bucket,
    cotf, actf, volf, pref, turned, w_one, w_two,
    r0, s1, r1, s2, r2,
    gpart, gsend, grecv, gx,
    load_sem, halo_send, halo_recv, b_send, b_recv, c_recv, g_send, g_recv,
):
    c1, width_x, width_y = raw_act.shape
    c0, c2 = raw_vol.shape[0], raw_cot.shape[0]
    dp = lax.axis_index("dp")
    sp = lax.axis_index("space")
    half = max(m // 2, 1)
    core, pos = lax.rem(sp, 2), sp // 2
    h = bucket.shape[0]
    whole = h // PARTS
    q = whole // half
    e = q // n
    gr = GROWS // m
    near, far = core * h, (1 - core) * h
    partner = (dp, sp + 1 - 2 * core)

    def in_space(other):
        return (dp, other)

    def in_dp(other):
        return (other, sp)

    def remote(src, dst, send, recv, device):
        return pltpu.make_async_remote_copy(
            src_ref=src, dst_ref=dst, send_sem=send, recv_sem=recv, device_id=device, device_id_type=MESH
        )

    if n * m > 1:
        barrier = pltpu.get_barrier_semaphore()

        @pl.loop(1, m)
        def _(o):
            pl.semaphore_signal(barrier, inc=1, device_id=in_space(lax.rem(sp + o, m)), device_id_type=MESH)

        @pl.loop(1, n)
        def _(o):
            pl.semaphore_signal(barrier, inc=1, device_id=in_dp(lax.rem(dp + o, n)), device_id_type=MESH)

    loads = [
        pltpu.make_async_copy(src, dst, load_sem.at[i])
        for i, (src, dst) in enumerate(
            (
                (cot_hbm, raw_cot), (vol_hbm, raw_vol), (act_hbm, raw_act),
                (two_hbm, two_v), (one_hbm, one_v), (bucket_hbm.at[pl.ds(near, h)], bucket),
            )
        )
    ]
    for load in loads:
        load.start()
    block = 16

    def center(raw, field, channels):
        @pl.loop(0, width_x // block)
        def _(step):
            x = step * block
            field[pl.ds(x + 1, block), channels : 2 * channels, :] = relaid(raw, x, block).astype(BF16)

    def spread(raw, field, channels):
        @pl.loop(0, width_x // block)
        def _(step):
            x = step * block
            value = relaid(raw, x, block).reshape(block * channels, LANES)
            for k in range(3):
                moved = value if k == 1 else shifted(value, k - 1)
                field[pl.ds(x + 1, block), k * channels : (k + 1) * channels, :] = moved.astype(BF16).reshape(
                    block, channels, LANES
                )

    def planes(field, low, high):
        depth = field.shape[1] // 3
        return [field.at[low + 1 : high + 1, p * depth : (p + 1) * depth, :] for p in range(3)]

    def send_halo(field, low, high, index):
        lower, own, upper = planes(field, low, high)

        @pl.when(sp < m - 1)
        def _():
            remote(own, lower, halo_send.at[index, 0], halo_recv.at[index, 0], in_space(lax.rem(sp + 1, m))).start()

        @pl.when(sp > 0)
        def _():
            remote(own, upper, halo_send.at[index, 1], halo_recv.at[index, 1], in_space(lax.rem(sp + m - 1, m))).start()

    def have_halo(field, low, high, index):
        lower, own, upper = planes(field, low, high)

        @pl.when(sp > 0)
        def _():
            landed(lower, halo_recv.at[index, 0])

        @pl.when(sp < m - 1)
        def _():
            landed(upper, halo_recv.at[index, 1])

    def sent_halo(field, low, high, index):
        lower, own, upper = planes(field, low, high)

        @pl.when(sp < m - 1)
        def _():
            landed(own, halo_send.at[index, 0])

        @pl.when(sp > 0)
        def _():
            landed(own, halo_send.at[index, 1])

    def blank(field):
        depth = field.shape[1] // 3
        for edge, p in ((0, 0), (m - 1, 2)):

            @pl.when(sp == edge)
            def _():
                @pl.loop(1, width_x + 1)
                def _(x):
                    field[x, p * depth : (p + 1) * depth, :] = jnp.zeros((depth, LANES), BF16)

    pieces = 4
    length = width_x // pieces
    raw_cuts = [(c * length, (c + 1) * length) for c in range(pieces)]
    pre_cuts = [
        (max(low - COUNT, 0), high if c == pieces - 1 else high - COUNT) for c, (low, high) in enumerate(raw_cuts)
    ]

    def first(t):
        at = t * whole
        remote(
            bucket_hbm.at[pl.ds(far + at, whole)], r0.at[pl.ds(at, whole)], b_send.at[t, 0], b_recv.at[t, 0], partner
        ).start()

    def second(t):
        at = t * whole
        if t == 0:
            loads[5].wait()
        landed(r0.at[pl.ds(at, whole)], b_recv.at[t, 0])
        part = min(32, whole)

        @pl.loop(0, whole // part)
        def _(step):
            some = pl.ds(at + step * part, part)
            value = bucket[some] + r0[some]
            bucket[some] = value
            s1[some] = value.astype(BF16)

        @pl.loop(1, half)
        def _(o):
            other = lax.rem(pos + o, half)
            remote(
                s1.at[pl.ds(at + other * q, q)], r1.at[t, o - 1],
                b_send.at[t, 1], b_recv.at[t, 1], in_space(other * 2 + core),
            ).start()

    def third(t):
        if half > 1:
            landed(r1.at[t], b_recv.at[t, 1])
        own = pl.ds(t * whole + pos * q, q)
        value = bucket[own]
        for o in range(1, half):
            value = value + r1[t, o - 1].astype(F32)
        bucket[own] = value
        s2[t] = value.astype(BF16)

        @pl.loop(1, n)
        def _(o):
            other = lax.rem(dp + o, n)
            remote(
                s2.at[t, pl.ds(other * e, e)], r2.at[t, o - 1], b_send.at[t, 2], b_recv.at[t, 2], in_dp(other)
            ).start()

    def fourth(t):
        landed(r2.at[t], b_recv.at[t, 2])
        value = bucket[pl.ds(t * whole + pos * q + dp * e, e)]
        for o in range(1, n):
            value = value + r2[t, o - 1].astype(F32)
        own = gath.at[pl.ds(near + t * whole + pos * q + dp * e, e)]
        own[...] = value.astype(BF16)

        @pl.loop(1, n)
        def _(o):
            remote(own, own, b_send.at[t, 3], b_recv.at[t, 3], in_dp(lax.rem(dp + o, n))).start()

    def share(t, chip):
        return gath.at[pl.ds(near + t * whole + chip * q, q)]

    def fifth(t):
        landed(gath.at[pl.ds(0, (n - 1) * e)], b_recv.at[t, 3])

        @pl.loop(1, half)
        def _(o):
            other = lax.rem(pos + o, half)
            remote(share(t, pos), share(t, pos), b_send.at[t, 4], c_recv.at[t, o - 1], in_space(other * 2 + core)).start()

        remote(share(t, pos), share(t, pos), b_send.at[t, 5], b_recv.at[t, 5], partner).start()

    def sixth(t):
        @pl.loop(1, half)
        def _(o):
            chip = lax.rem(pos + half - o, half)
            landed(share(t, chip), c_recv.at[t, o - 1])
            remote(share(t, chip), share(t, chip), b_send.at[t, 5], b_recv.at[t, 5], partner).start()

    if n * m > 1:
        pl.semaphore_wait(barrier, m - 1 + n - 1)

    def clear():
        for field in (cotf, actf, volf, pref):
            for slot in (0, width_x + 1):
                field[slot] = jnp.zeros(field.shape[1:], BF16)
        gpart[...] = jnp.zeros(gpart.shape, F32)
        blank(cotf)
        blank(volf)
        blank(pref)

    def load_cot():
        loads[0].wait()
        center(raw_cot, cotf, c2)
        for c, (low, high) in enumerate(raw_cuts):
            send_halo(cotf, low, high, c)

    def load_vol():
        loads[1].wait()
        center(raw_vol, volf, c0)
        send_halo(volf, 0, width_x, 2 * pieces)

    def load_act():
        loads[2].wait()
        spread(raw_act, actf, c1)

    def load_weights():
        loads[3].wait()
        weights(two_v, w_two, c1)
        loads[4].wait()
        weights(one_v, w_one, c0)

    def convolve_one(c):
        low, high = pre_cuts[c]
        have_halo(cotf, *raw_cuts[c], c)

        @pl.loop(0, (high - low) // COUNT)
        def _(step):
            x = low + step * COUNT
            for u, value in enumerate(convolved(cotf, w_two, x, COUNT, c1)):
                slope = jnp.where(actf[x + u + 1, c1 : 2 * c1, :].astype(F32) > 0, 1.0, 0.2)
                value = (value * slope).astype(BF16)
                pref[x + u + 1, c1 : 2 * c1, :] = value
                wide = value.astype(F32)
                turned[x + u, :c1, :] = shifted(wide, 1).astype(BF16)
                turned[x + u, c1 : 2 * c1, :] = value
                turned[x + u, 2 * c1 :, :] = shifted(wide, -1).astype(BF16)

        send_halo(pref, low, high, pieces + c)

    def terms_two(c):
        kernel_terms(actf, cotf, 1, gpart, 0, *raw_cuts[c], UNROLL)

    def terms_one():
        have_halo(volf, 0, width_x, 2 * pieces)
        kernel_terms(volf, turned, 0, gpart, 9 * c1, 0, width_x, UNROLL)

    def convolve_two():
        for c in range(pieces):
            have_halo(pref, *pre_cuts[c], pieces + c)

        @pl.loop(0, width_x // COUNT)
        def _(step):
            x = step * COUNT
            for u, value in enumerate(convolved(pref, w_one, x, COUNT, c0)):
                gin[x + u] = value.astype(BF16)

    def gradients_cut():
        gsend[...] = gpart[...].astype(gsend.dtype)

        @pl.loop(1, m)
        def _(o):
            other = lax.rem(sp + o, m)
            remote(
                gsend.at[pl.ds(pl.multiple_of(other * gr, gr), gr), :], grecv.at[o - 1],
                g_send.at[0], g_recv.at[0], in_space(other),
            ).start()

    def gradients_swap():
        landed(grecv, g_recv.at[0])
        value = gpart[pl.ds(pl.multiple_of(sp * gr, gr), gr), :]
        for o in range(1, m):
            value = value + grecv[o - 1].astype(F32)
        gx[dp] = value.astype(gx.dtype)

        @pl.loop(1, n)
        def _(o):
            remote(gx.at[dp], gx.at[dp], g_send.at[1], g_recv.at[1], in_dp(lax.rem(dp + o, n))).start()

    def gradients_join():
        landed(gx.at[pl.ds(0, n - 1)], g_recv.at[1])
        value = gx[0].astype(F32)
        for d in range(1, n):
            value = value + gx[d].astype(F32)
        own_g = gfull.at[pl.ds(pl.multiple_of(sp * gr, gr), gr), :]
        own_g[...] = (value * scale).astype(gfull.dtype)

        @pl.loop(1, m)
        def _(o):
            remote(own_g, own_g, g_send.at[2], g_recv.at[2], in_space(lax.rem(sp + o, m))).start()

    first(0)
    first(1)
    load_cot()
    second(0)
    second(1)
    clear()
    load_vol()
    load_act()
    load_weights()
    convolve_one(0)
    terms_two(0)
    convolve_one(1)
    terms_two(1)
    third(0)
    convolve_one(2)
    terms_two(2)
    third(1)
    convolve_one(3)
    terms_two(3)
    terms_one()
    gradients_cut()
    fourth(0)
    fourth(1)
    gradients_swap()
    fifth(0)
    fifth(1)
    gradients_join()
    convolve_two()
    sixth(0)
    sixth(1)

    if m > 1:
        landed(gfull.at[pl.ds(0, (m - 1) * gr), :], g_recv.at[2])
        for t in range(PARTS):
            landed(gath.at[pl.ds(0, whole)], b_recv.at[t, 5])

        for c in range(pieces):
            sent_halo(cotf, *raw_cuts[c], c)
            sent_halo(pref, *pre_cuts[c], pieces + c)
        sent_halo(volf, 0, width_x, 2 * pieces)
        for t in range(PARTS):
            landed(r0.at[pl.ds(0, whole)], b_send.at[t, 0])
            if half > 1:
                landed(r1.at[t], b_send.at[t, 1])
                landed(gath.at[pl.ds(0, (half - 1) * q)], b_send.at[t, 4])
            landed(r2.at[t], b_send.at[t, 2])
            landed(gath.at[pl.ds(0, (n - 1) * e)], b_send.at[t, 3])
            landed(gath.at[pl.ds(0, whole)], b_send.at[t, 5])
        landed(grecv, g_send.at[0])
        landed(gx.at[pl.ds(0, n - 1)], g_send.at[1])
        landed(gfull.at[pl.ds(0, (m - 1) * gr), :], g_send.at[2])


def finish(gin, gfull, gath, gin_hbm, g1_hbm, g2_hbm, bsum_hbm, gin_v, g1_v, g2_v, bsum_v, sem):
    width_x, c0, _ = gin.shape
    c1, c2 = g2_v.shape[1:]
    rows = gath.shape[0]
    count = 8
    part = rows // count
    copies = []
    for t in range(count):
        at = pl.ds(t * part, part)
        bsum_v[at] = gath[at].astype(F32)
        copies.append(pltpu.make_async_copy(bsum_v.at[at], bsum_hbm.at[at], sem.at[t]))
        copies[-1].start()
    block = 16
    for t in range(width_x // block):
        at = pl.ds(t * block, block)
        gin_v[:, at, :] = jnp.transpose(gin[at].astype(F32), (1, 0, 2)).astype(BF16)
    copies.append(pltpu.make_async_copy(gin_v, gin_hbm, sem.at[count]))
    copies[-1].start()
    for j in range(3):
        for k in range(3):
            for p in range(3):
                row = (j * 3 + k) * c1
                g2_v[(2 - p) * 9 + j * 3 + k] = gfull[row : row + c1, p * c2 : (p + 1) * c2].astype(F32)
                row = 9 * c1 + (j * 3 + p) * c0
                g1_v[p * 9 + j * 3 + k] = gfull[row : row + c0, k * c1 : (k + 1) * c1].astype(F32)
    copies.append(pltpu.make_async_copy(g2_v, g2_hbm, sem.at[count + 1]))
    copies.append(pltpu.make_async_copy(g1_v, g1_hbm, sem.at[count + 2]))
    copies[-2].start()
    copies[-1].start()
    for copy in copies:
        copy.wait()


def call(n, m, scale, vol, act, cot, one, two, bucket):
    c0, width_x, width_y = vol.shape
    c1, c2 = act.shape[0], cot.shape[0]
    rows = bucket.shape[0]
    half = max(m // 2, 1)
    h = rows // 2
    q = h // PARTS // half
    e = q // n
    gr = GROWS // m
    wire = BF16
    tile = (TILE, LANES)
    vmem = pltpu.VMEM
    dma = pltpu.SemaphoreType.DMA
    tall = width_x + 2
    scratch = [
        vmem((c0, width_x, width_y), BF16), vmem((c1, width_x, width_y), BF16), vmem((c2, width_x, width_y), BF16),
        vmem((27, c0, c1), BF16), vmem((27, c1, c2), BF16), vmem((h, *tile), F32),
        vmem((tall, 3 * c2, LANES), BF16), vmem((tall, 3 * c1, LANES), BF16),
        vmem((tall, 3 * c0, LANES), BF16), vmem((tall, 3 * c1, LANES), BF16),
        vmem((width_x, 3 * c1, LANES), BF16),
        vmem((3 * c0, 9 * c1), BF16), vmem((3 * c1, 9 * c2), BF16),
        vmem((h, *tile), F32), vmem((h, *tile), BF16),
        vmem((PARTS, max(half - 1, 1), q, *tile), BF16), vmem((PARTS, q, *tile), BF16),
        vmem((PARTS, max(n - 1, 1), e, *tile), BF16),
        vmem((GROWS, LANES), F32), vmem((GROWS, LANES), wire), vmem((max(m - 1, 1), gr, LANES), wire),
        vmem((n, gr, LANES), wire),
        dma((6,)), dma((9, 2)), dma((9, 2)), dma((PARTS, 6)), dma((PARTS, 6)), dma((PARTS, max(half - 1, 1))),
        dma((3,)), dma((3,)),
    ]
    hbm = pl.BlockSpec(memory_space=pltpu.HBM)
    local = pl.BlockSpec(memory_space=pltpu.VMEM)
    cells = width_x * width_y
    operands = [pltpu.with_memory_space_constraint(v, pltpu.HBM) for v in (vol, act, cot, one, two, bucket)]
    gin, gfull, gath = pl.pallas_call(
        functools.partial(kernel, n, m, scale),
        out_shape=(
            jax.ShapeDtypeStruct((width_x, c0, width_y), BF16),
            jax.ShapeDtypeStruct((GROWS, LANES), wire),
            jax.ShapeDtypeStruct((rows, *tile), BF16),
        ),
        in_specs=[hbm] * 6,
        out_specs=(local,) * 3,
        scratch_shapes=scratch,
        compiler_params=pltpu.CompilerParams(
            collective_id=0 if n * m > 1 else None, has_side_effects=True, vmem_limit_bytes=VMEM_LIMIT
        ),
        cost_estimate=pl.CostEstimate(
            flops=4 * 27 * cells * c1 * (c0 + c2), bytes_accessed=8 << 20, transcendentals=0
        ),
    )(*operands)
    return pl.pallas_call(
        finish,
        out_shape=(
            jax.ShapeDtypeStruct((c0, width_x, width_y), BF16),
            jax.ShapeDtypeStruct((27, c0, c1), F32),
            jax.ShapeDtypeStruct((27, c1, c2), F32),
            jax.ShapeDtypeStruct((rows, *tile), F32),
        ),
        in_specs=[local] * 3,
        out_specs=(hbm,) * 4,
        scratch_shapes=[
            vmem((c0, width_x, width_y), BF16), vmem((27, c0, c1), F32), vmem((27, c1, c2), F32),
            vmem((rows, *tile), F32), dma((11,)),
        ],
        compiler_params=pltpu.CompilerParams(vmem_limit_bytes=VMEM_LIMIT),
        cost_estimate=pl.CostEstimate(flops=0, bytes_accessed=5 << 20, transcendentals=0),
    )(gin, gfull, gath)


def per_device(n, m, volume_in, hidden_act, out_cot, kernel_one, kernel_two, grad_bucket):
    width_x, width_y = volume_in.shape[3:]
    scale = 1.0 / math.sqrt(volume_in.shape[0] * n * volume_in.shape[1] * m * width_x * width_y)
    gin, g1, g2, bsum = call(
        n, m, scale,
        volume_in[0, 0], hidden_act[0, 0], out_cot[0, 0],
        kernel_one.reshape((27,) + kernel_one.shape[3:]), kernel_two.reshape((27,) + kernel_two.shape[3:]),
        grad_bucket.reshape(-1, TILE, LANES),
    )
    return (gin[None, None], g1.reshape(kernel_one.shape), g2.reshape(kernel_two.shape), bsum.reshape(-1))


def solution(mesh):
    fields = P("dp", "space", None, None, None)
    return jax.shard_map(
        functools.partial(per_device, mesh.shape["dp"], mesh.shape["space"]),
        mesh=mesh,
        in_specs=(fields, fields, fields, P(), P(), P(("dp", "space"), None)),
        out_specs=(fields, P(), P(), P()),
        check_vma=False,
    )
```

```python
import functools
import math

import jax
import jax.numpy as jnp
from jax import lax
from jax.experimental import pallas as pl
from jax.experimental.pallas import tpu as pltpu
from jax.sharding import PartitionSpec as P

MESH = pl.DeviceIdType.MESH
F32 = jnp.float32
BF16 = jnp.bfloat16
LANES = 128
GROWS = 512
UNROLL = 16
COUNT = 8
PARTS = 2
TILE = 8
VMEM_LIMIT = 40 << 20


def landed(ref, sem):
    pltpu.make_async_copy(ref, ref, sem).wait()


def shifted(value, step):
    width = value.shape[-1]
    lane = lax.broadcasted_iota(jnp.int32, value.shape, value.ndim - 1)
    if step < 0:
        return jnp.where(lane >= 1, pltpu.roll(value, 1, value.ndim - 1), 0.0)
    return jnp.where(lane < width - 1, pltpu.roll(value, width - 1, value.ndim - 1), 0.0)


def relaid(raw, start, count):
    return jnp.transpose(raw[:, pl.ds(start, count), :].astype(F32), (1, 0, 2))


def weights(kernel, out, channels):
    for k in range(3):
        pieces = [
            kernel[(2 - p) * 9 + (2 - j) * 3 + (2 - k)].astype(F32) for j in range(3) for p in range(3)
        ]
        out[k * channels : (k + 1) * channels, :] = jnp.concatenate(pieces, axis=1).astype(BF16)


def convolved(field, weight, x, count, channels):
    rows = weight.shape[1]
    columns = [field[pl.ds(x + u, 3)].reshape(rows, LANES) for u in range(count)]
    product = jnp.dot(weight[...], jnp.concatenate(columns, axis=1), preferred_element_type=F32)
    out = []
    for u in range(count):
        value = product[:, u * LANES : (u + 1) * LANES]
        out.append(
            value[channels : 2 * channels]
            + shifted(value[:channels], -1)
            + shifted(value[2 * channels :], 1)
        )
    return out


def kernel_terms(left, right, offset, out, first, low, high, unroll):
    @pl.loop(0, (high - low) // unroll)
    def _(step):
        add_terms(left, right, offset, out, first, low + step * unroll, unroll)


def add_terms(left, right, offset, out, first, x, unroll):
    rows = 3 * left.shape[1]
    depth = right.shape[1]
    a = jnp.concatenate([left[pl.ds(x + u, 3)].reshape(rows, LANES) for u in range(unroll)], axis=1)
    b = jnp.concatenate([right[x + u + offset] for u in range(unroll)], axis=1)
    out[first : first + rows, :depth] += lax.dot_general(
        a, b, (((1,), (1,)), ((), ())), preferred_element_type=F32
    )


def kernel(
    n, m, scale,
    vol_hbm, act_hbm, cot_hbm, one_hbm, two_hbm, bucket_hbm,
    gin, gfull, gath,
    raw_vol, raw_act, raw_cot, one_v, two_v, bucket,
    cotf, actf, volf, pref, turned, w_one, w_two,
    r0, s1, r1, s2, r2,
    gpart, gsend, grecv, gx,
    load_sem, halo_send, halo_recv, b_send, b_recv, c_recv, g_send, g_recv,
):
    c1, width_x, width_y = raw_act.shape
    c0, c2 = raw_vol.shape[0], raw_cot.shape[0]
    dp = lax.axis_index("dp")
    sp = lax.axis_index("space")
    half = max(m // 2, 1)
    core, pos = lax.rem(sp, 2), sp // 2
    h = bucket.shape[0]
    whole = h // PARTS
    q = whole // half
    e = q // n
    gr = GROWS // n
    near, far = core * h, (1 - core) * h
    partner = (dp, sp + 1 - 2 * core)

    def in_space(other):
        return (dp, other)

    def in_dp(other):
        return (other, sp)

    def remote(src, dst, send, recv, device):
        return pltpu.make_async_remote_copy(
            src_ref=src, dst_ref=dst, send_sem=send, recv_sem=recv, device_id=device, device_id_type=MESH
        )

    if n * m > 1:
        barrier = pltpu.get_barrier_semaphore()

        @pl.loop(1, m)
        def _(o):
            pl.semaphore_signal(barrier, inc=1, device_id=in_space(lax.rem(sp + o, m)), device_id_type=MESH)

        @pl.loop(1, n)
        def _(o):
            pl.semaphore_signal(barrier, inc=1, device_id=in_dp(lax.rem(dp + o, n)), device_id_type=MESH)

    loads = [
        pltpu.make_async_copy(src, dst, load_sem.at[i])
        for i, (src, dst) in enumerate(
            (
                (cot_hbm, raw_cot), (vol_hbm, raw_vol), (act_hbm, raw_act),
                (two_hbm, two_v), (one_hbm, one_v), (bucket_hbm.at[pl.ds(near, h)], bucket),
            )
        )
    ]
    for load in loads:
        load.start()
    block = 16

    def center(raw, field, channels):
        @pl.loop(0, width_x // block)
        def _(step):
            x = step * block
            field[pl.ds(x + 1, block), channels : 2 * channels, :] = relaid(raw, x, block).astype(BF16)

    def spread(raw, field, channels):
        @pl.loop(0, width_x // block)
        def _(step):
            x = step * block
            value = relaid(raw, x, block).reshape(block * channels, LANES)
            for k in range(3):
                moved = value if k == 1 else shifted(value, k - 1)
                field[pl.ds(x + 1, block), k * channels : (k + 1) * channels, :] = moved.astype(BF16).reshape(
                    block, channels, LANES
                )

    def planes(field, low, high):
        depth = field.shape[1] // 3
        return [field.at[low + 1 : high + 1, p * depth : (p + 1) * depth, :] for p in range(3)]

    def send_halo(field, low, high, index):
        lower, own, upper = planes(field, low, high)

        @pl.when(sp < m - 1)
        def _():
            remote(own, lower, halo_send.at[index, 0], halo_recv.at[index, 0], in_space(lax.rem(sp + 1, m))).start()

        @pl.when(sp > 0)
        def _():
            remote(own, upper, halo_send.at[index, 1], halo_recv.at[index, 1], in_space(lax.rem(sp + m - 1, m))).start()

    def have_halo(field, low, high, index):
        lower, own, upper = planes(field, low, high)

        @pl.when(sp > 0)
        def _():
            landed(lower, halo_recv.at[index, 0])

        @pl.when(sp < m - 1)
        def _():
            landed(upper, halo_recv.at[index, 1])

    def sent_halo(field, low, high, index):
        lower, own, upper = planes(field, low, high)

        @pl.when(sp < m - 1)
        def _():
            landed(own, halo_send.at[index, 0])

        @pl.when(sp > 0)
        def _():
            landed(own, halo_send.at[index, 1])

    def blank(field):
        depth = field.shape[1] // 3
        for edge, p in ((0, 0), (m - 1, 2)):

            @pl.when(sp == edge)
            def _():
                @pl.loop(1, width_x + 1)
                def _(x):
                    field[x, p * depth : (p + 1) * depth, :] = jnp.zeros((depth, LANES), BF16)

    pieces = 4
    length = width_x // pieces
    raw_cuts = [(c * length, (c + 1) * length) for c in range(pieces)]
    pre_cuts = [
        (max(low - COUNT, 0), high if c == pieces - 1 else high - COUNT) for c, (low, high) in enumerate(raw_cuts)
    ]

    def first(t):
        at = t * whole
        remote(
            bucket_hbm.at[pl.ds(far + at, whole)], r0.at[pl.ds(at, whole)], b_send.at[t, 0], b_recv.at[t, 0], partner
        ).start()

    def second(t):
        at = t * whole
        if t == 0:
            loads[5].wait()
        landed(r0.at[pl.ds(at, whole)], b_recv.at[t, 0])
        part = min(32, whole)

        @pl.loop(0, whole // part)
        def _(step):
            some = pl.ds(at + step * part, part)
            value = bucket[some] + r0[some]
            bucket[some] = value
            s1[some] = value.astype(BF16)

        @pl.loop(1, half)
        def _(o):
            other = lax.rem(pos + o, half)
            remote(
                s1.at[pl.ds(at + other * q, q)], r1.at[t, o - 1],
                b_send.at[t, 1], b_recv.at[t, 1], in_space(other * 2 + core),
            ).start()

    def third(t):
        if half > 1:
            landed(r1.at[t], b_recv.at[t, 1])
        own = pl.ds(t * whole + pos * q, q)
        value = bucket[own]
        for o in range(1, half):
            value = value + r1[t, o - 1].astype(F32)
        bucket[own] = value
        s2[t] = value.astype(BF16)

        @pl.loop(1, n)
        def _(o):
            other = lax.rem(dp + o, n)
            remote(
                s2.at[t, pl.ds(other * e, e)], r2.at[t, o - 1], b_send.at[t, 2], b_recv.at[t, 2], in_dp(other)
            ).start()

    def fourth(t):
        landed(r2.at[t], b_recv.at[t, 2])
        value = bucket[pl.ds(t * whole + pos * q + dp * e, e)]
        for o in range(1, n):
            value = value + r2[t, o - 1].astype(F32)
        own = gath.at[pl.ds(near + t * whole + pos * q + dp * e, e)]
        own[...] = value.astype(BF16)

        @pl.loop(1, n)
        def _(o):
            remote(own, own, b_send.at[t, 3], b_recv.at[t, 3], in_dp(lax.rem(dp + o, n))).start()

    def share(t, chip):
        return gath.at[pl.ds(near + t * whole + chip * q, q)]

    def fifth(t):
        landed(gath.at[pl.ds(0, (n - 1) * e)], b_recv.at[t, 3])

        @pl.loop(1, half)
        def _(o):
            other = lax.rem(pos + o, half)
            remote(share(t, pos), share(t, pos), b_send.at[t, 4], c_recv.at[t, o - 1], in_space(other * 2 + core)).start()

        remote(share(t, pos), share(t, pos), b_send.at[t, 5], b_recv.at[t, 5], partner).start()

    def sixth(t):
        @pl.loop(1, half)
        def _(o):
            chip = lax.rem(pos + half - o, half)
            landed(share(t, chip), c_recv.at[t, o - 1])
            remote(share(t, chip), share(t, chip), b_send.at[t, 5], b_recv.at[t, 5], partner).start()

    if n * m > 1:
        pl.semaphore_wait(barrier, m - 1 + n - 1)

    def clear():
        for field in (cotf, actf, volf, pref):
            for slot in (0, width_x + 1):
                field[slot] = jnp.zeros(field.shape[1:], BF16)
        gpart[...] = jnp.zeros(gpart.shape, F32)
        blank(cotf)
        blank(volf)
        blank(pref)

    def load_cot():
        loads[0].wait()
        center(raw_cot, cotf, c2)
        for c, (low, high) in enumerate(raw_cuts):
            send_halo(cotf, low, high, c)

    def load_vol():
        loads[1].wait()
        center(raw_vol, volf, c0)
        send_halo(volf, 0, width_x, 2 * pieces)

    def load_act():
        loads[2].wait()
        spread(raw_act, actf, c1)

    def load_weights():
        loads[3].wait()
        weights(two_v, w_two, c1)
        loads[4].wait()
        weights(one_v, w_one, c0)

    def convolve_one(c):
        low, high = pre_cuts[c]
        have_halo(cotf, *raw_cuts[c], c)

        @pl.loop(0, (high - low) // COUNT)
        def _(step):
            x = low + step * COUNT
            add_terms(actf, cotf, 1, gpart, 0, x, COUNT)
            for u, value in enumerate(convolved(cotf, w_two, x, COUNT, c1)):
                slope = jnp.where(actf[x + u + 1, c1 : 2 * c1, :].astype(F32) > 0, 1.0, 0.2)
                value = (value * slope).astype(BF16)
                pref[x + u + 1, c1 : 2 * c1, :] = value
                wide = value.astype(F32)
                turned[x + u, :c1, :] = shifted(wide, 1).astype(BF16)
                turned[x + u, c1 : 2 * c1, :] = value
                turned[x + u, 2 * c1 :, :] = shifted(wide, -1).astype(BF16)

        send_halo(pref, low, high, pieces + c)

    def terms_one():
        have_halo(volf, 0, width_x, 2 * pieces)
        kernel_terms(volf, turned, 0, gpart, 9 * c1, 0, width_x, UNROLL)

    def convolve_two():
        for c in range(pieces):
            have_halo(pref, *pre_cuts[c], pieces + c)

        @pl.loop(0, width_x // COUNT)
        def _(step):
            x = step * COUNT
            for u, value in enumerate(convolved(pref, w_one, x, COUNT, c0)):
                gin[x + u] = value.astype(BF16)

    def gradients_cut():
        gsend[...] = gpart[...].astype(gsend.dtype)

        @pl.loop(1, n)
        def _(o):
            other = lax.rem(dp + o, n)
            remote(
                gsend.at[pl.ds(pl.multiple_of(other * gr, gr), gr), :], grecv.at[o - 1],
                g_send.at[0], g_recv.at[0], in_dp(other),
            ).start()

    def gradients_swap():
        landed(grecv, g_recv.at[0])
        value = gpart[pl.ds(pl.multiple_of(dp * gr, gr), gr), :]
        for o in range(1, n):
            value = value + grecv[o - 1].astype(F32)
        gx[sp] = value.astype(gx.dtype)

        @pl.loop(1, m)
        def _(o):
            remote(gx.at[sp], gx.at[sp], g_send.at[1], g_recv.at[1], in_space(lax.rem(sp + o, m))).start()

    def gradients_join():
        landed(gx.at[pl.ds(0, m - 1)], g_recv.at[1])
        value = gx[0].astype(F32)
        for d in range(1, m):
            value = value + gx[d].astype(F32)
        own_g = gfull.at[pl.ds(pl.multiple_of(dp * gr, gr), gr), :]
        own_g[...] = (value * scale).astype(gfull.dtype)

        @pl.loop(1, n)
        def _(o):
            remote(own_g, own_g, g_send.at[2], g_recv.at[2], in_dp(lax.rem(dp + o, n))).start()

    first(0)
    first(1)
    load_cot()
    second(0)
    second(1)
    clear()
    load_vol()
    load_act()
    load_weights()
    convolve_one(0)
    convolve_one(1)
    third(0)
    convolve_one(2)
    third(1)
    convolve_one(3)
    terms_one()
    gradients_cut()
    fourth(0)
    fourth(1)
    gradients_swap()
    fifth(0)
    fifth(1)
    gradients_join()
    convolve_two()
    sixth(0)
    sixth(1)

    if m > 1:
        landed(gfull.at[pl.ds(0, (n - 1) * gr), :], g_recv.at[2])
        for t in range(PARTS):
            landed(gath.at[pl.ds(0, whole)], b_recv.at[t, 5])

        for c in range(pieces):
            sent_halo(cotf, *raw_cuts[c], c)
            sent_halo(pref, *pre_cuts[c], pieces + c)
        sent_halo(volf, 0, width_x, 2 * pieces)
        for t in range(PARTS):
            landed(r0.at[pl.ds(0, whole)], b_send.at[t, 0])
            if half > 1:
                landed(r1.at[t], b_send.at[t, 1])
                landed(gath.at[pl.ds(0, (half - 1) * q)], b_send.at[t, 4])
            landed(r2.at[t], b_send.at[t, 2])
            landed(gath.at[pl.ds(0, (n - 1) * e)], b_send.at[t, 3])
            landed(gath.at[pl.ds(0, whole)], b_send.at[t, 5])
        landed(grecv, g_send.at[0])
        landed(gx.at[pl.ds(0, m - 1)], g_send.at[1])
        landed(gfull.at[pl.ds(0, (n - 1) * gr), :], g_send.at[2])


def finish(gin, gfull, gath, gin_hbm, g1_hbm, g2_hbm, bsum_hbm, gin_v, g1_v, g2_v, bsum_v, sem):
    width_x, c0, _ = gin.shape
    c1, c2 = g2_v.shape[1:]
    rows = gath.shape[0]
    count = 8
    part = rows // count
    copies = []
    for t in range(count):
        at = pl.ds(t * part, part)
        bsum_v[at] = gath[at].astype(F32)
        copies.append(pltpu.make_async_copy(bsum_v.at[at], bsum_hbm.at[at], sem.at[t]))
        copies[-1].start()
    block = 16
    for t in range(width_x // block):
        at = pl.ds(t * block, block)
        gin_v[:, at, :] = jnp.transpose(gin[at].astype(F32), (1, 0, 2)).astype(BF16)
    copies.append(pltpu.make_async_copy(gin_v, gin_hbm, sem.at[count]))
    copies[-1].start()
    for j in range(3):
        for k in range(3):
            for p in range(3):
                row = (j * 3 + k) * c1
                g2_v[(2 - p) * 9 + j * 3 + k] = gfull[row : row + c1, p * c2 : (p + 1) * c2].astype(F32)
                row = 9 * c1 + (j * 3 + p) * c0
                g1_v[p * 9 + j * 3 + k] = gfull[row : row + c0, k * c1 : (k + 1) * c1].astype(F32)
    copies.append(pltpu.make_async_copy(g2_v, g2_hbm, sem.at[count + 1]))
    copies.append(pltpu.make_async_copy(g1_v, g1_hbm, sem.at[count + 2]))
    copies[-2].start()
    copies[-1].start()
    for copy in copies:
        copy.wait()


def call(n, m, scale, vol, act, cot, one, two, bucket):
    c0, width_x, width_y = vol.shape
    c1, c2 = act.shape[0], cot.shape[0]
    rows = bucket.shape[0]
    half = max(m // 2, 1)
    h = rows // 2
    q = h // PARTS // half
    e = q // n
    gr = GROWS // n
    wire = BF16
    tile = (TILE, LANES)
    vmem = pltpu.VMEM
    dma = pltpu.SemaphoreType.DMA
    tall = width_x + 2
    scratch = [
        vmem((c0, width_x, width_y), BF16), vmem((c1, width_x, width_y), BF16), vmem((c2, width_x, width_y), BF16),
        vmem((27, c0, c1), BF16), vmem((27, c1, c2), BF16), vmem((h, *tile), F32),
        vmem((tall, 3 * c2, LANES), BF16), vmem((tall, 3 * c1, LANES), BF16),
        vmem((tall, 3 * c0, LANES), BF16), vmem((tall, 3 * c1, LANES), BF16),
        vmem((width_x, 3 * c1, LANES), BF16),
        vmem((3 * c0, 9 * c1), BF16), vmem((3 * c1, 9 * c2), BF16),
        vmem((h, *tile), F32), vmem((h, *tile), BF16),
        vmem((PARTS, max(half - 1, 1), q, *tile), BF16), vmem((PARTS, q, *tile), BF16),
        vmem((PARTS, max(n - 1, 1), e, *tile), BF16),
        vmem((GROWS, LANES), F32), vmem((GROWS, LANES), wire), vmem((max(n - 1, 1), gr, LANES), wire),
        vmem((m, gr, LANES), wire),
        dma((6,)), dma((9, 2)), dma((9, 2)), dma((PARTS, 6)), dma((PARTS, 6)), dma((PARTS, max(half - 1, 1))),
        dma((3,)), dma((3,)),
    ]
    hbm = pl.BlockSpec(memory_space=pltpu.HBM)
    local = pl.BlockSpec(memory_space=pltpu.VMEM)
    cells = width_x * width_y
    operands = [pltpu.with_memory_space_constraint(v, pltpu.HBM) for v in (vol, act, cot, one, two, bucket)]
    gin, gfull, gath = pl.pallas_call(
        functools.partial(kernel, n, m, scale),
        out_shape=(
            jax.ShapeDtypeStruct((width_x, c0, width_y), BF16),
            jax.ShapeDtypeStruct((GROWS, LANES), wire),
            jax.ShapeDtypeStruct((rows, *tile), BF16),
        ),
        in_specs=[hbm] * 6,
        out_specs=(local,) * 3,
        scratch_shapes=scratch,
        compiler_params=pltpu.CompilerParams(
            collective_id=0 if n * m > 1 else None, has_side_effects=True, vmem_limit_bytes=VMEM_LIMIT
        ),
        cost_estimate=pl.CostEstimate(
            flops=4 * 27 * cells * c1 * (c0 + c2), bytes_accessed=8 << 20, transcendentals=0
        ),
    )(*operands)
    return pl.pallas_call(
        finish,
        out_shape=(
            jax.ShapeDtypeStruct((c0, width_x, width_y), BF16),
            jax.ShapeDtypeStruct((27, c0, c1), F32),
            jax.ShapeDtypeStruct((27, c1, c2), F32),
            jax.ShapeDtypeStruct((rows, *tile), F32),
        ),
        in_specs=[local] * 3,
        out_specs=(hbm,) * 4,
        scratch_shapes=[
            vmem((c0, width_x, width_y), BF16), vmem((27, c0, c1), F32), vmem((27, c1, c2), F32),
            vmem((rows, *tile), F32), dma((11,)),
        ],
        compiler_params=pltpu.CompilerParams(vmem_limit_bytes=VMEM_LIMIT),
        cost_estimate=pl.CostEstimate(flops=0, bytes_accessed=5 << 20, transcendentals=0),
    )(gin, gfull, gath)


def per_device(n, m, volume_in, hidden_act, out_cot, kernel_one, kernel_two, grad_bucket):
    width_x, width_y = volume_in.shape[3:]
    scale = 1.0 / math.sqrt(volume_in.shape[0] * n * volume_in.shape[1] * m * width_x * width_y)
    gin, g1, g2, bsum = call(
        n, m, scale,
        volume_in[0, 0], hidden_act[0, 0], out_cot[0, 0],
        kernel_one.reshape((27,) + kernel_one.shape[3:]), kernel_two.reshape((27,) + kernel_two.shape[3:]),
        grad_bucket.reshape(-1, TILE, LANES),
    )
    return (gin[None, None], g1.reshape(kernel_one.shape), g2.reshape(kernel_two.shape), bsum.reshape(-1))


def solution(mesh):
    fields = P("dp", "space", None, None, None)
    return jax.shard_map(
        functools.partial(per_device, mesh.shape["dp"], mesh.shape["space"]),
        mesh=mesh,
        in_specs=(fields, fields, fields, P(), P(), P(("dp", "space"), None)),
        out_specs=(fields, P(), P(), P()),
        check_vma=False,
    )
```

```python
import functools
import math

import jax
import jax.numpy as jnp
from jax import lax
from jax.experimental import pallas as pl
from jax.experimental.pallas import tpu as pltpu
from jax.sharding import PartitionSpec as P

MESH = pl.DeviceIdType.MESH
F32 = jnp.float32
BF16 = jnp.bfloat16
LANES = 128
GROWS = 512
UNROLL = 32
COUNT = 8
PARTS = 2
TILE = 8
VMEM_LIMIT = 40 << 20


def landed(ref, sem):
    pltpu.make_async_copy(ref, ref, sem).wait()


def shifted(value, step):
    width = value.shape[-1]
    lane = lax.broadcasted_iota(jnp.int32, value.shape, value.ndim - 1)
    if step < 0:
        return jnp.where(lane >= 1, pltpu.roll(value, 1, value.ndim - 1), 0.0)
    return jnp.where(lane < width - 1, pltpu.roll(value, width - 1, value.ndim - 1), 0.0)


def relaid(raw, start, count):
    return jnp.transpose(raw[:, pl.ds(start, count), :].astype(F32), (1, 0, 2))


def weights(kernel, out, channels):
    for k in range(3):
        pieces = [
            kernel[(2 - p) * 9 + (2 - j) * 3 + (2 - k)].astype(F32) for j in range(3) for p in range(3)
        ]
        out[k * channels : (k + 1) * channels, :] = jnp.concatenate(pieces, axis=1).astype(BF16)


def convolved(field, weight, x, count, channels):
    rows = weight.shape[1]
    columns = [field[pl.ds(x + u, 3)].reshape(rows, LANES) for u in range(count)]
    product = jnp.dot(weight[...], jnp.concatenate(columns, axis=1), preferred_element_type=F32)
    out = []
    for u in range(count):
        value = product[:, u * LANES : (u + 1) * LANES]
        out.append(
            value[channels : 2 * channels]
            + shifted(value[:channels], -1)
            + shifted(value[2 * channels :], 1)
        )
    return out


def kernel_terms(left, right, offset, out, first, low, high, unroll):
    @pl.loop(0, (high - low) // unroll)
    def _(step):
        add_terms(left, right, offset, out, first, low + step * unroll, unroll)


def add_terms(left, right, offset, out, first, x, unroll):
    rows = 3 * left.shape[1]
    depth = right.shape[1]
    a = jnp.concatenate([left[pl.ds(x + u, 3)].reshape(rows, LANES) for u in range(unroll)], axis=1)
    b = jnp.concatenate([right[x + u + offset] for u in range(unroll)], axis=1)
    out[first : first + rows, :depth] += lax.dot_general(
        a, b, (((1,), (1,)), ((), ())), preferred_element_type=F32
    )


def kernel(
    n, m, scale,
    vol_hbm, act_hbm, cot_hbm, one_hbm, two_hbm, bucket_hbm,
    gin, gfull, gath,
    raw_vol, raw_act, raw_cot, one_v, two_v, bucket,
    cotf, actf, volf, pref, turned, w_one, w_two,
    r0, s1, r1, s2, r2,
    gpart, gsend, grecv, gx,
    load_sem, halo_send, halo_recv, b_send, b_recv, c_recv, g_send, g_recv,
):
    c1, width_x, width_y = raw_act.shape
    c0, c2 = raw_vol.shape[0], raw_cot.shape[0]
    dp = lax.axis_index("dp")
    sp = lax.axis_index("space")
    half = max(m // 2, 1)
    core, pos = lax.rem(sp, 2), sp // 2
    h = bucket.shape[0]
    whole = h // PARTS
    q = whole // half
    e = q // n
    gr = GROWS // n
    near, far = core * h, (1 - core) * h
    partner = (dp, sp + 1 - 2 * core)

    def in_space(other):
        return (dp, other)

    def in_dp(other):
        return (other, sp)

    def remote(src, dst, send, recv, device):
        return pltpu.make_async_remote_copy(
            src_ref=src, dst_ref=dst, send_sem=send, recv_sem=recv, device_id=device, device_id_type=MESH
        )

    if n * m > 1:
        barrier = pltpu.get_barrier_semaphore()

        @pl.loop(1, m)
        def _(o):
            pl.semaphore_signal(barrier, inc=1, device_id=in_space(lax.rem(sp + o, m)), device_id_type=MESH)

        @pl.loop(1, n)
        def _(o):
            pl.semaphore_signal(barrier, inc=1, device_id=in_dp(lax.rem(dp + o, n)), device_id_type=MESH)

    loads = [
        pltpu.make_async_copy(src, dst, load_sem.at[i])
        for i, (src, dst) in enumerate(
            (
                (cot_hbm, raw_cot), (vol_hbm, raw_vol), (act_hbm, raw_act),
                (two_hbm, two_v), (one_hbm, one_v), (bucket_hbm.at[pl.ds(near, h)], bucket),
            )
        )
    ]
    for load in loads:
        load.start()
    block = 16

    def center(raw, field, channels):
        @pl.loop(0, width_x // block)
        def _(step):
            x = step * block
            field[pl.ds(x + 1, block), channels : 2 * channels, :] = relaid(raw, x, block).astype(BF16)

    def spread(raw, field, channels):
        @pl.loop(0, width_x // block)
        def _(step):
            x = step * block
            value = relaid(raw, x, block).reshape(block * channels, LANES)
            for k in range(3):
                moved = value if k == 1 else shifted(value, k - 1)
                field[pl.ds(x + 1, block), k * channels : (k + 1) * channels, :] = moved.astype(BF16).reshape(
                    block, channels, LANES
                )

    def planes(field, low, high):
        depth = field.shape[1] // 3
        return [field.at[low + 1 : high + 1, p * depth : (p + 1) * depth, :] for p in range(3)]

    def send_halo(field, low, high, index):
        lower, own, upper = planes(field, low, high)

        @pl.when(sp < m - 1)
        def _():
            remote(own, lower, halo_send.at[index, 0], halo_recv.at[index, 0], in_space(lax.rem(sp + 1, m))).start()

        @pl.when(sp > 0)
        def _():
            remote(own, upper, halo_send.at[index, 1], halo_recv.at[index, 1], in_space(lax.rem(sp + m - 1, m))).start()

    def have_halo(field, low, high, index):
        lower, own, upper = planes(field, low, high)

        @pl.when(sp > 0)
        def _():
            landed(lower, halo_recv.at[index, 0])

        @pl.when(sp < m - 1)
        def _():
            landed(upper, halo_recv.at[index, 1])

    def sent_halo(field, low, high, index):
        lower, own, upper = planes(field, low, high)

        @pl.when(sp < m - 1)
        def _():
            landed(own, halo_send.at[index, 0])

        @pl.when(sp > 0)
        def _():
            landed(own, halo_send.at[index, 1])

    def blank(field):
        depth = field.shape[1] // 3
        for edge, p in ((0, 0), (m - 1, 2)):

            @pl.when(sp == edge)
            def _():
                @pl.loop(1, width_x + 1)
                def _(x):
                    field[x, p * depth : (p + 1) * depth, :] = jnp.zeros((depth, LANES), BF16)

    pieces = 4
    length = width_x // pieces
    raw_cuts = [(c * length, (c + 1) * length) for c in range(pieces)]
    pre_cuts = [
        (max(low - COUNT, 0), high if c == pieces - 1 else high - COUNT) for c, (low, high) in enumerate(raw_cuts)
    ]

    def first(t):
        at = t * whole
        remote(
            bucket_hbm.at[pl.ds(far + at, whole)], r0.at[pl.ds(at, whole)], b_send.at[t, 0], b_recv.at[t, 0], partner
        ).start()

    def second(t):
        at = t * whole
        if t == 0:
            loads[5].wait()
        landed(r0.at[pl.ds(at, whole)], b_recv.at[t, 0])
        part = min(32, whole)

        @pl.loop(0, whole // part)
        def _(step):
            some = pl.ds(at + step * part, part)
            value = bucket[some] + r0[some]
            bucket[some] = value
            s1[some] = value.astype(BF16)

        @pl.loop(1, half)
        def _(o):
            other = lax.rem(pos + o, half)
            remote(
                s1.at[pl.ds(at + other * q, q)], r1.at[t, o - 1],
                b_send.at[t, 1], b_recv.at[t, 1], in_space(other * 2 + core),
            ).start()

    def third(t):
        if half > 1:
            landed(r1.at[t], b_recv.at[t, 1])
        own = pl.ds(t * whole + pos * q, q)
        value = bucket[own]
        for o in range(1, half):
            value = value + r1[t, o - 1].astype(F32)
        bucket[own] = value
        s2[t] = value.astype(BF16)

        @pl.loop(1, n)
        def _(o):
            other = lax.rem(dp + o, n)
            remote(
                s2.at[t, pl.ds(other * e, e)], r2.at[t, o - 1], b_send.at[t, 2], b_recv.at[t, 2], in_dp(other)
            ).start()

    def fourth(t):
        landed(r2.at[t], b_recv.at[t, 2])
        value = bucket[pl.ds(t * whole + pos * q + dp * e, e)]
        for o in range(1, n):
            value = value + r2[t, o - 1].astype(F32)
        own = gath.at[pl.ds(near + t * whole + pos * q + dp * e, e)]
        own[...] = value.astype(BF16)

        @pl.loop(1, n)
        def _(o):
            remote(own, own, b_send.at[t, 3], b_recv.at[t, 3], in_dp(lax.rem(dp + o, n))).start()

    def share(t, chip):
        return gath.at[pl.ds(near + t * whole + chip * q, q)]

    def fifth(t):
        landed(gath.at[pl.ds(0, (n - 1) * e)], b_recv.at[t, 3])

        @pl.loop(1, half)
        def _(o):
            other = lax.rem(pos + o, half)
            remote(share(t, pos), share(t, pos), b_send.at[t, 4], c_recv.at[t, o - 1], in_space(other * 2 + core)).start()

        remote(share(t, pos), share(t, pos), b_send.at[t, 5], b_recv.at[t, 5], partner).start()

    def sixth(t):
        @pl.loop(1, half)
        def _(o):
            chip = lax.rem(pos + half - o, half)
            landed(share(t, chip), c_recv.at[t, o - 1])
            remote(share(t, chip), share(t, chip), b_send.at[t, 5], b_recv.at[t, 5], partner).start()

    if n * m > 1:
        pl.semaphore_wait(barrier, m - 1 + n - 1)

    def clear():
        for field in (cotf, actf, volf, pref):
            for slot in (0, width_x + 1):
                field[slot] = jnp.zeros(field.shape[1:], BF16)
        gpart[...] = jnp.zeros(gpart.shape, F32)
        blank(cotf)
        blank(volf)
        blank(pref)

    def load_cot():
        loads[0].wait()
        center(raw_cot, cotf, c2)
        for c, (low, high) in enumerate(raw_cuts):
            send_halo(cotf, low, high, c)

    def load_vol():
        loads[1].wait()
        center(raw_vol, volf, c0)
        send_halo(volf, 0, width_x, 2 * pieces)

    def load_act():
        loads[2].wait()
        spread(raw_act, actf, c1)

    def load_weights():
        loads[3].wait()
        weights(two_v, w_two, c1)
        loads[4].wait()
        weights(one_v, w_one, c0)

    def convolve_one(c):
        low, high = pre_cuts[c]
        have_halo(cotf, *raw_cuts[c], c)

        @pl.loop(0, (high - low) // COUNT)
        def _(step):
            x = low + step * COUNT
            add_terms(actf, cotf, 1, gpart, 0, x, COUNT)
            for u, value in enumerate(convolved(cotf, w_two, x, COUNT, c1)):
                slope = jnp.where(actf[x + u + 1, c1 : 2 * c1, :].astype(F32) > 0, 1.0, 0.2)
                value = (value * slope).astype(BF16)
                pref[x + u + 1, c1 : 2 * c1, :] = value
                wide = value.astype(F32)
                turned[x + u, :c1, :] = shifted(wide, 1).astype(BF16)
                turned[x + u, c1 : 2 * c1, :] = value
                turned[x + u, 2 * c1 :, :] = shifted(wide, -1).astype(BF16)

        send_halo(pref, low, high, pieces + c)

    def terms_one():
        have_halo(volf, 0, width_x, 2 * pieces)
        kernel_terms(volf, turned, 0, gpart, 9 * c1, 0, width_x, UNROLL)

    def convolve_two():
        for c in range(pieces):
            have_halo(pref, *pre_cuts[c], pieces + c)

        @pl.loop(0, width_x // COUNT)
        def _(step):
            x = step * COUNT
            for u, value in enumerate(convolved(pref, w_one, x, COUNT, c0)):
                gin[x + u] = value.astype(BF16)

    def gradients_cut():
        gsend[...] = gpart[...].astype(gsend.dtype)

        @pl.loop(1, n)
        def _(o):
            other = lax.rem(dp + o, n)
            remote(
                gsend.at[pl.ds(pl.multiple_of(other * gr, gr), gr), :], grecv.at[o - 1],
                g_send.at[0], g_recv.at[0], in_dp(other),
            ).start()

    def gradients_swap():
        landed(grecv, g_recv.at[0])
        value = gpart[pl.ds(pl.multiple_of(dp * gr, gr), gr), :]
        for o in range(1, n):
            value = value + grecv[o - 1].astype(F32)
        gx[sp] = value.astype(gx.dtype)

        @pl.loop(1, m)
        def _(o):
            remote(gx.at[sp], gx.at[sp], g_send.at[1], g_recv.at[1], in_space(lax.rem(sp + o, m))).start()

    def gradients_join():
        landed(gx.at[pl.ds(0, m - 1)], g_recv.at[1])
        value = gx[0].astype(F32)
        for d in range(1, m):
            value = value + gx[d].astype(F32)
        own_g = gfull.at[pl.ds(pl.multiple_of(dp * gr, gr), gr), :]
        own_g[...] = (value * scale).astype(gfull.dtype)

        @pl.loop(1, n)
        def _(o):
            remote(own_g, own_g, g_send.at[2], g_recv.at[2], in_dp(lax.rem(dp + o, n))).start()

    first(0)
    first(1)
    load_cot()
    second(0)
    second(1)
    clear()
    load_vol()
    load_act()
    load_weights()
    convolve_one(0)
    convolve_one(1)
    third(0)
    convolve_one(2)
    third(1)
    convolve_one(3)
    terms_one()
    gradients_cut()
    fourth(0)
    fourth(1)
    gradients_swap()
    fifth(0)
    fifth(1)
    gradients_join()
    convolve_two()
    sixth(0)
    sixth(1)

    if m > 1:
        landed(gfull.at[pl.ds(0, (n - 1) * gr), :], g_recv.at[2])
        for t in range(PARTS):
            landed(gath.at[pl.ds(0, whole)], b_recv.at[t, 5])

        for c in range(pieces):
            sent_halo(cotf, *raw_cuts[c], c)
            sent_halo(pref, *pre_cuts[c], pieces + c)
        sent_halo(volf, 0, width_x, 2 * pieces)
        for t in range(PARTS):
            landed(r0.at[pl.ds(0, whole)], b_send.at[t, 0])
            if half > 1:
                landed(r1.at[t], b_send.at[t, 1])
                landed(gath.at[pl.ds(0, (half - 1) * q)], b_send.at[t, 4])
            landed(r2.at[t], b_send.at[t, 2])
            landed(gath.at[pl.ds(0, (n - 1) * e)], b_send.at[t, 3])
            landed(gath.at[pl.ds(0, whole)], b_send.at[t, 5])
        landed(grecv, g_send.at[0])
        landed(gx.at[pl.ds(0, m - 1)], g_send.at[1])
        landed(gfull.at[pl.ds(0, (n - 1) * gr), :], g_send.at[2])


def finish(gin, gfull, gath, gin_hbm, g1_hbm, g2_hbm, bsum_hbm, gin_v, g1_v, g2_v, bsum_v, sem):
    width_x, c0, _ = gin.shape
    c1, c2 = g2_v.shape[1:]
    rows = gath.shape[0]
    count = 8
    part = rows // count
    copies = []
    for t in range(count):
        at = pl.ds(t * part, part)
        bsum_v[at] = gath[at].astype(F32)
        copies.append(pltpu.make_async_copy(bsum_v.at[at], bsum_hbm.at[at], sem.at[t]))
        copies[-1].start()
    block = 16
    for t in range(width_x // block):
        at = pl.ds(t * block, block)
        gin_v[:, at, :] = jnp.transpose(gin[at].astype(F32), (1, 0, 2)).astype(BF16)
    copies.append(pltpu.make_async_copy(gin_v, gin_hbm, sem.at[count]))
    copies[-1].start()
    for j in range(3):
        for k in range(3):
            for p in range(3):
                row = (j * 3 + k) * c1
                g2_v[(2 - p) * 9 + j * 3 + k] = gfull[row : row + c1, p * c2 : (p + 1) * c2].astype(F32)
                row = 9 * c1 + (j * 3 + p) * c0
                g1_v[p * 9 + j * 3 + k] = gfull[row : row + c0, k * c1 : (k + 1) * c1].astype(F32)
    copies.append(pltpu.make_async_copy(g2_v, g2_hbm, sem.at[count + 1]))
    copies.append(pltpu.make_async_copy(g1_v, g1_hbm, sem.at[count + 2]))
    copies[-2].start()
    copies[-1].start()
    for copy in copies:
        copy.wait()


def call(n, m, scale, vol, act, cot, one, two, bucket):
    c0, width_x, width_y = vol.shape
    c1, c2 = act.shape[0], cot.shape[0]
    rows = bucket.shape[0]
    half = max(m // 2, 1)
    h = rows // 2
    q = h // PARTS // half
    e = q // n
    gr = GROWS // n
    wire = BF16
    tile = (TILE, LANES)
    vmem = pltpu.VMEM
    dma = pltpu.SemaphoreType.DMA
    tall = width_x + 2
    scratch = [
        vmem((c0, width_x, width_y), BF16), vmem((c1, width_x, width_y), BF16), vmem((c2, width_x, width_y), BF16),
        vmem((27, c0, c1), BF16), vmem((27, c1, c2), BF16), vmem((h, *tile), F32),
        vmem((tall, 3 * c2, LANES), BF16), vmem((tall, 3 * c1, LANES), BF16),
        vmem((tall, 3 * c0, LANES), BF16), vmem((tall, 3 * c1, LANES), BF16),
        vmem((width_x, 3 * c1, LANES), BF16),
        vmem((3 * c0, 9 * c1), BF16), vmem((3 * c1, 9 * c2), BF16),
        vmem((h, *tile), F32), vmem((h, *tile), BF16),
        vmem((PARTS, max(half - 1, 1), q, *tile), BF16), vmem((PARTS, q, *tile), BF16),
        vmem((PARTS, max(n - 1, 1), e, *tile), BF16),
        vmem((GROWS, LANES), F32), vmem((GROWS, LANES), wire), vmem((max(n - 1, 1), gr, LANES), wire),
        vmem((m, gr, LANES), wire),
        dma((6,)), dma((9, 2)), dma((9, 2)), dma((PARTS, 6)), dma((PARTS, 6)), dma((PARTS, max(half - 1, 1))),
        dma((3,)), dma((3,)),
    ]
    hbm = pl.BlockSpec(memory_space=pltpu.HBM)
    local = pl.BlockSpec(memory_space=pltpu.VMEM)
    cells = width_x * width_y
    operands = [pltpu.with_memory_space_constraint(v, pltpu.HBM) for v in (vol, act, cot, one, two, bucket)]
    gin, gfull, gath = pl.pallas_call(
        functools.partial(kernel, n, m, scale),
        out_shape=(
            jax.ShapeDtypeStruct((width_x, c0, width_y), BF16),
            jax.ShapeDtypeStruct((GROWS, LANES), wire),
            jax.ShapeDtypeStruct((rows, *tile), BF16),
        ),
        in_specs=[hbm] * 6,
        out_specs=(local,) * 3,
        scratch_shapes=scratch,
        compiler_params=pltpu.CompilerParams(
            collective_id=0 if n * m > 1 else None, has_side_effects=True, vmem_limit_bytes=VMEM_LIMIT
        ),
        cost_estimate=pl.CostEstimate(
            flops=4 * 27 * cells * c1 * (c0 + c2), bytes_accessed=8 << 20, transcendentals=0
        ),
    )(*operands)
    return pl.pallas_call(
        finish,
        out_shape=(
            jax.ShapeDtypeStruct((c0, width_x, width_y), BF16),
            jax.ShapeDtypeStruct((27, c0, c1), F32),
            jax.ShapeDtypeStruct((27, c1, c2), F32),
            jax.ShapeDtypeStruct((rows, *tile), F32),
        ),
        in_specs=[local] * 3,
        out_specs=(hbm,) * 4,
        scratch_shapes=[
            vmem((c0, width_x, width_y), BF16), vmem((27, c0, c1), F32), vmem((27, c1, c2), F32),
            vmem((rows, *tile), F32), dma((11,)),
        ],
        compiler_params=pltpu.CompilerParams(vmem_limit_bytes=VMEM_LIMIT),
        cost_estimate=pl.CostEstimate(flops=0, bytes_accessed=5 << 20, transcendentals=0),
    )(gin, gfull, gath)


def per_device(n, m, volume_in, hidden_act, out_cot, kernel_one, kernel_two, grad_bucket):
    width_x, width_y = volume_in.shape[3:]
    scale = 1.0 / math.sqrt(volume_in.shape[0] * n * volume_in.shape[1] * m * width_x * width_y)
    gin, g1, g2, bsum = call(
        n, m, scale,
        volume_in[0, 0], hidden_act[0, 0], out_cot[0, 0],
        kernel_one.reshape((27,) + kernel_one.shape[3:]), kernel_two.reshape((27,) + kernel_two.shape[3:]),
        grad_bucket.reshape(-1, TILE, LANES),
    )
    return (gin[None, None], g1.reshape(kernel_one.shape), g2.reshape(kernel_two.shape), bsum.reshape(-1))


def solution(mesh):
    fields = P("dp", "space", None, None, None)
    return jax.shard_map(
        functools.partial(per_device, mesh.shape["dp"], mesh.shape["space"]),
        mesh=mesh,
        in_specs=(fields, fields, fields, P(), P(), P(("dp", "space"), None)),
        out_specs=(fields, P(), P(), P()),
        check_vma=False,
    )
```
